256 devices in a mesh: chan: 64 (over z, y, core), stn: 4 (over x).
Axes of the slice: x: 4, y: 4, z: 8, core: 2. Of those that a mesh axis runs over, the one named last changes fastest.
Arguments:
- visibilities: bfloat16 [2, 256, 512, 512], P(None, 'chan', 'stn'), may hold values from -140 to 140
- calibrator: float32 [256], P('chan'), may hold values from 20 to 40
- catalog: float32 [5, 65536], P(None, 'chan'), may hold values from -2 to 2, as said below
- assignment: int32 [65536, 1], replicated, may hold values from 0 to 63; in each aligned block of 1024 rows (0 to 1023, 1024 to 2047, ...) at most 32 rows name the same one
- stations: float32 [2, 512], replicated, may hold values from -150 to 150
- input_order: int32 [512], replicated, may hold values from 0 to 511, each once
- station_flags: int32 [512], replicated, may hold values 0 or 1
Outputs:
- gains: float32 [2, 256, 512], P(None, 'chan', 'stn')
- residual: bfloat16 [2, 256, 512, 512], P(None, 'chan', 'stn')
- changes: float32 [3, 256], P(None, 'chan')
The draws below stay inside these ranges and needn't reach their ends.
Inputs may be any that keep to these rules, and one draw needn't show every extreme that they name: `assignment`: of the 1024 sources on one index of chan, at most 32 belong to any one channel block. `catalog`: rows l and m lie within -0.1 to 0.1, flux within 0.02 to 0.5, spectral index within -1.2 to 0.2, curvature within -2 to 2.
All inputs are finite; a program needn't handle non-finite values.
Results may differ from the reference program's by a relative error of at most 0.0039.
Values sent between devices are 32-bit elements; how exact they have to be, the bound alone decides.
No kernel may reach another device: no remote copies, remote signals or barrier semaphores. Data moves between devices by JAX's collectives and lax.ppermute only.
A program may use at most 64 MiB of HBM per device.

```python
import math
import jax
import jax.numpy as jnp
import numpy as np
from jax import lax

NST = 512
SRC_DEV = 1024
CH_DEV = 4
ITERS = 3
NCH = 256
SRC_ALL = 65536
CAP = 32
N_CHAN = 64


def draw_visibilities(key, part):
    keys = jax.random.split(jax.random.fold_in(key, 11), 3)
    amplitude = jnp.exp(jax.random.uniform(keys[0], (NCH, NST), jnp.float32, jnp.log(0.7), jnp.log(1.4)))
    angle_part = jax.random.uniform(keys[1], (NCH, NST), jnp.float32, -0.6, 0.6)
    noise_part = 6.0 * jnp.clip(jax.random.normal(keys[2], (2, NCH, NST, NST), jnp.float32), -6.0, 6.0)
    gain_real = amplitude * jnp.cos(angle_part)
    gain_imag = amplitude * jnp.sin(angle_part)
    real_part = 30.0 * (gain_real[:, :, None] * gain_real[:, None, :] + gain_imag[:, :, None] * gain_imag[:, None, :]) + noise_part[0]
    imag_part = 30.0 * (gain_imag[:, :, None] * gain_real[:, None, :] - gain_real[:, :, None] * gain_imag[:, None, :]) + noise_part[1]
    return jnp.stack([real_part, imag_part]).astype(jnp.bfloat16)


def draw_catalog(key, part):
    keys = jax.random.split(jax.random.fold_in(key, 23), 4)
    spots = jax.random.uniform(keys[0], (2, SRC_ALL), jnp.float32, -0.1, 0.1)
    flux = jnp.exp(jax.random.uniform(keys[1], (SRC_ALL,), jnp.float32, jnp.log(0.02), jnp.log(0.5)))
    slope = jax.random.uniform(keys[2], (SRC_ALL,), jnp.float32, -1.0, 0.0)
    bend = jax.random.uniform(keys[3], (SRC_ALL,), jnp.float32, -1.5, 1.5)
    return jnp.concatenate([spots, flux[None, :], slope[None, :], bend[None, :]], axis=0)


def place_ends(values, rng, smallest, top_value):
    longest = values.shape.index(max(values.shape))
    spots = []
    for shift in (0, 1):
        where = [jax.random.randint(jax.random.fold_in(rng, axis), (), 0, length) for axis, length in enumerate(values.shape)]
        where[longest] = (where[longest] + shift) % values.shape[longest]
        spots.append(tuple(where))
    return values.at[spots[0]].set(smallest).at[spots[1]].set(top_value)


def level_of(key, shape, shards, least, top_value):
    gain, own = 1.0, jax.random.fold_in(key, 6)
    for dim, shards_of in shards:
        steps = jnp.exp(jax.random.uniform(jax.random.fold_in(own, dim), (shards_of,), jnp.float32, least / len(shards), top_value / len(shards)))
        gain = gain * jnp.repeat(steps, shape[dim] // shards_of).reshape([-1 if axis == dim else 1 for axis in range(len(shape))])
    return gain


def routed_block(stream_key, own, number, rows, amount, top, most, lean):
    order = jax.random.permutation(stream_key, amount)
    heavy_load, usual = portions_of(amount, rows * top, most, lean, True), portions_of(amount, rows * top, most, lean, False)
    places = jnp.arange(amount)

    def named(sizes, rotation):
        used = int((sizes > 0).sum())
        fixed = max(1, used // 4)
        moved = fixed + (places - fixed + rotation * (used - fixed)) % max(1, amount - fixed)
        return jnp.zeros((amount,), jnp.int32).at[order[jnp.where(places < fixed, places, moved)]].set(jnp.asarray(sizes, jnp.int32))

    sizes = jnp.where(number % 4 == 0, named(heavy_load, number // 4), named(usual, number - number // 4 - 1))
    mixed = jax.random.permutation(jax.random.fold_in(own, 3), amount)
    giver, sink = mixed[0:amount // 2 * 2:2], mixed[1:amount // 2 * 2:2]
    room = jnp.minimum(sizes[giver] - 1, most - sizes[sink]) // 2
    room = jnp.where((giver == order[0]) | (sink == order[0]) | (sizes[sink] == 0), 0, jnp.maximum(room, 0))
    moved = jax.random.randint(jax.random.fold_in(own, 4), (amount // 2,), 0, 1 << 20) % (room + 1)
    sizes = sizes.at[giver].add(-moved).at[sink].add(moved)
    members = jnp.searchsorted(jnp.cumsum(sizes), jnp.arange(rows * top), side="right").astype(jnp.int32)
    grid = members.reshape(top, rows).T
    grid = grid[jax.random.permutation(jax.random.fold_in(own, 1), rows)]
    rotation = jax.random.randint(jax.random.fold_in(own, 2), (rows, 1), 0, top)
    return jnp.take_along_axis(grid, (jnp.arange(top)[None, :] + rotation) % top, axis=1)


def portions_of(count, total, limit, skew, full):
    weights = [(1 << 20) // math.isqrt(rank ** skew) + 1 for rank in range(1, count + 1)]
    largest = limit if full else min(limit, max(-(-total // count), total * weights[0] // sum(weights)))
    least = 1 if total - largest >= count - 1 else 0
    holding, rest = [largest] + [least] * (count - 1), total - largest - least * (count - 1)
    while rest > 0:
        candidates = [i for i in range(1, count) if holding[i] < largest] or [i for i in range(1, count) if holding[i] < limit]
        whole, remaining = sum([weights[i] for i in candidates]), rest
        for i in candidates:
            addition = min(limit - holding[i], max(1, remaining * weights[i] // whole), rest)
            holding[i] = holding[i] + addition
            rest = rest - addition
    return np.array(holding)


def setup_inputs(seed: int = 0) -> dict:
    key_list = jax.random.split(jax.random.key(seed), 8)
    visibilities = draw_visibilities(jax.random.fold_in(key_list[7], 71), 0)
    calibrator = jnp.clip(jnp.exp(math.log(40.0) - 0.6931472 * jax.random.uniform(key_list[1], (NCH,), jnp.float32) ** level_of(key_list[1], (NCH,), ((0, 64),), -0.2, 0.2)), 20.0, 40.0)
    catalog = draw_catalog(jax.random.fold_in(key_list[7], 71), 0)
    assignment_keys = jax.random.split(jax.random.fold_in(key_list[3], 1), SRC_ALL // SRC_DEV)
    assignment_turns = jax.random.permutation(jax.random.fold_in(key_list[3], 3), SRC_ALL // SRC_DEV)
    assignment = jax.vmap(lambda own, number: routed_block(jax.random.fold_in(key_list[3], 2), own, number, SRC_DEV, N_CHAN, 1, CAP, 1))(assignment_keys, assignment_turns).reshape((SRC_ALL, 1))
    stations = jnp.clip(jax.random.uniform(key_list[4], (2, NST), jnp.float32, -150.0, 150.0), -150.0, 150.0)
    input_order = jax.random.permutation(key_list[5], NST).astype(jnp.int32)
    station_flags = place_ends((jax.random.randint(key_list[6], (NST,), 0, 16) < 15).astype(jnp.int32), jax.random.fold_in(key_list[6], 1), 0, 1)
    return dict(visibilities=visibilities, calibrator=calibrator, catalog=catalog, assignment=assignment, stations=stations, input_order=input_order, station_flags=station_flags)


def slot_table(assigned):
    source_total = assigned.shape[0]
    blocks = jnp.arange(N_CHAN, dtype=jnp.int32)
    onehot = (assigned[:, None] == blocks[None, :]).astype(jnp.int32)
    running = jnp.cumsum(onehot.reshape(N_CHAN, SRC_DEV, N_CHAN), axis=1).astype(jnp.int32).reshape(source_total, N_CHAN)
    ranking = jnp.sum(onehot * running, axis=1).astype(jnp.int32) - 1
    anchor = jnp.arange(source_total, dtype=jnp.int32) // SRC_DEV
    position = (anchor * CAP + ranking).astype(jnp.int32)
    source_slot = jnp.full((N_CHAN, N_CHAN * CAP), source_total, jnp.int32)
    return source_slot.at[assigned, position].set(jnp.arange(source_total, dtype=jnp.int32))


def predict(components, placed, frequency, bright_centre):
    phase_angle = (2.0 * jnp.pi * frequency) * (components[0][:, None] * placed[0][None, :] + components[1][:, None] * placed[1][None, :])
    cosine = jnp.cos(phase_angle)
    sine_part = jnp.sin(phase_angle)
    log_freq = jnp.log(frequency)
    brightness = components[2] * jnp.exp(log_freq * (components[3] + components[4] * log_freq))
    right_side = jnp.concatenate([brightness[:, None] * cosine, brightness[:, None] * sine_part], axis=0).astype(jnp.bfloat16)
    cos_rows = cosine.astype(jnp.bfloat16)
    sin_rows = sine_part.astype(jnp.bfloat16)
    left_side = jnp.concatenate([jnp.concatenate([cos_rows, sin_rows], axis=0), jnp.concatenate([sin_rows, -cos_rows], axis=0)], axis=1)
    model_full = lax.dot_general(left_side.astype(jnp.float32), right_side.astype(jnp.float32), (((0,), (0,)), ((), ())), precision=lax.Precision.HIGHEST, preferred_element_type=jnp.float32)
    station_count = placed.shape[1]
    return model_full[:station_count] + bright_centre, model_full[station_count:]


def reference(visibilities, calibrator, catalog, assignment, stations, input_order, station_flags):
    station_count = visibilities.shape[2]
    source_total = catalog.shape[1]
    source_slot = slot_table(assignment[:, 0])
    padded = jnp.concatenate([catalog, jnp.zeros((5, 1), jnp.float32)], axis=1)
    placed = stations[:, input_order]
    station_ok = station_flags[input_order].astype(jnp.float32)
    indices = jnp.arange(station_count, dtype=jnp.int32)
    pair_weight = station_ok[:, None] * station_ok[None, :] * (indices[:, None] != indices[None, :]).astype(jnp.float32)

    def one_channel(inputs):
        channel, vis_pair, bright_centre = inputs
        components = padded[:, source_slot[channel // CH_DEV]]
        frequency = 1.0 + 0.5 * channel.astype(jnp.float32) / NCH
        model_real, model_imag = predict(components, placed, frequency, bright_centre)
        vis_real = vis_pair[0].astype(jnp.float32)
        vis_imag = vis_pair[1].astype(jnp.float32)
        gain_real = jnp.ones((station_count,), jnp.float32)
        gain_imag = jnp.zeros((station_count,), jnp.float32)
        history = []
        for iteration in range(ITERS):
            weight_real = gain_real[None, :] * model_real + gain_imag[None, :] * model_imag
            weight_imag = gain_real[None, :] * model_imag - gain_imag[None, :] * model_real
            top_real = jnp.sum(pair_weight * (weight_real * vis_real + weight_imag * vis_imag), axis=1)
            top_imag = jnp.sum(pair_weight * (weight_real * vis_imag - weight_imag * vis_real), axis=1)
            bottom = jnp.sum(pair_weight * (weight_real * weight_real + weight_imag * weight_imag), axis=1) + 1e-6 + (1.0 - station_ok)
            new_real = top_real / bottom
            new_imag = top_imag / bottom
            if iteration % 2 == 1:
                new_real = 0.5 * (new_real + gain_real)
                new_imag = 0.5 * (new_imag + gain_imag)
            norm_moved = jnp.sum((new_real - gain_real) ** 2 + (new_imag - gain_imag) ** 2)
            norm_total = jnp.sum(new_real * new_real + new_imag * new_imag)
            history.append(norm_moved / (norm_total + 1e-6))
            gain_real = new_real
            gain_imag = new_imag
        pair_real = gain_real[:, None] * gain_real[None, :] + gain_imag[:, None] * gain_imag[None, :]
        pair_imag = gain_imag[:, None] * gain_real[None, :] - gain_real[:, None] * gain_imag[None, :]
        res_real = pair_weight * (vis_real - (pair_real * model_real - pair_imag * model_imag))
        res_imag = pair_weight * (vis_imag - (pair_real * model_imag + pair_imag * model_real))
        return jnp.stack([gain_real, gain_imag]), jnp.stack([res_real, res_imag]).astype(jnp.bfloat16), jnp.stack(history)

    channels = jnp.arange(NCH, dtype=jnp.int32)
    by_channel = jnp.moveaxis(visibilities, 1, 0)
    gain_all, resid_all, change_all = lax.map(one_channel, (channels, by_channel, calibrator))
    return jnp.moveaxis(gain_all, 0, 1), jnp.moveaxis(resid_all, 0, 1), jnp.moveaxis(change_all, 0, 1)
```

```python
import jax
import jax.numpy as jnp
from jax import lax
from jax.experimental import pallas as pl
from jax.experimental.pallas import tpu as pltpu
from jax.sharding import PartitionSpec as P

ITERS = 3
CAP = 32
VMEM = pltpu.VMEM
F32 = jnp.float32
BF16 = jnp.bfloat16
NT = (((1,), (1,)), ((), ()))

SIN_HALF = (3.141582005383235, -5.167142124470761, 2.541892570102862, -0.5546189642693115)
COS_HALF = (
    0.999999953374577,
    -4.934792843915727,
    4.05841155956257,
    -1.3318775116821093,
    0.2196907395767838,
)
SIN_STEP = (1.9999932214850844, -0.33258196069982343)
COS_STEP = (1.9999999959214183, -0.9999979659209961, 0.08318303377955542)
ROUND = 12582912.0


def horner(coefficients, x):
    total = coefficients[-1]
    for c in coefficients[-2::-1]:
        total = total * x + c
    return total


def split3(x):
    high = x.astype(BF16).astype(F32)
    rest = x - high
    middle = rest.astype(BF16).astype(F32)
    return high, middle, rest - middle


def spread_kernel(vis_ref, *out_refs):
    k = lax.axis_index("stn")
    for s in range(4):
        out_refs[s][...] = vis_ref[:, lax.rem(k + s, 4)].astype(F32)


def route_kernel(assign_ref, cat_ref, st_ref, order_ref, flag_ref, send_ref, xb_ref, yb_ref, ok_ref, own, sem):
    c = lax.axis_index("chan")
    copy = pltpu.make_async_copy(assign_ref.at[pl.ds(pl.multiple_of(c * 8, 8), 8)], own, sem)
    copy.start()
    n = order_ref.shape[1]
    hot = (lax.broadcasted_iota(jnp.int32, (n, n), 0) == order_ref[...]).astype(F32).astype(BF16)
    high, middle, low = split3(st_ref[...])
    rows = jnp.concatenate([high, middle, low, flag_ref[...].astype(F32), jnp.zeros((9, n), F32)], axis=0)
    placed = jnp.dot(rows.astype(BF16), hot, preferred_element_type=F32)
    middle_nu = 1.0 + (4.0 * c.astype(F32) + 1.5) * (1.0 / 512.0)
    x = (placed[0:1] + placed[2:3] + placed[4:5]) * middle_nu
    y = (placed[1:2] + placed[3:4] + placed[5:6]) * middle_nu
    ok_ref[...] = jnp.broadcast_to(placed[6:7], ok_ref.shape)
    for b in range(n // 128):
        cols = slice(128 * b, 128 * b + 128)
        xb_ref[cols] = jnp.broadcast_to(x[:, cols], (128, 128)).T
        yb_ref[cols] = jnp.broadcast_to(y[:, cols], (128, 128)).T
    copy.wait()
    blocks = lax.broadcasted_iota(jnp.int32, (64, 128), 0)
    hits = [(blocks == own[t : t + 1]).astype(F32) for t in range(8)]
    stacked = jnp.concatenate(hits, axis=0).astype(BF16)
    upper = lax.broadcasted_iota(jnp.int32, (128, 128), 0) <= lax.broadcasted_iota(jnp.int32, (128, 128), 1)
    running = jnp.dot(stacked, upper.astype(F32).astype(BF16), preferred_element_type=F32)
    totals = jnp.dot(stacked, jnp.ones((128, 128), BF16), preferred_element_type=F32)
    before = jnp.full((64, 128), -1.0, F32)
    slot = lax.broadcasted_iota(jnp.int32, (CAP, 128), 0).astype(F32)
    pieces = split3(cat_ref[...])
    left, right = [], []
    for t in range(8):
        part = slice(64 * t, 64 * t + 64)
        rank = jnp.sum(hits[t] * (running[part] + before), axis=0, keepdims=True)
        before = before + totals[part]
        chosen = slot == rank
        hit = hits[t].astype(BF16)
        for piece in pieces:
            left.append(hit)
            here = piece[:, 128 * t : 128 * t + 128]
            right.append(
                jnp.concatenate([jnp.where(chosen, here[f : f + 1], 0.0) for f in range(5)], axis=0).astype(BF16)
            )
    sent = lax.dot_general(
        jnp.concatenate(left, axis=1), jnp.concatenate(right, axis=1), NT, preferred_element_type=F32
    )
    send_ref[:, 0, :] = sent


def phasor_kernel(comp_ref, xb_ref, yb_ref, right_ref, left_ref, model_ref, wide, mine):
    width = comp_ref.shape[1]
    c = lax.axis_index("chan")
    k = lax.axis_index("stn")
    rows = mine.shape[0]
    quarter = rows // 4
    base = 1.0 + 4.0 * c.astype(F32) * (1.0 / 512.0)
    middle_nu = 1.0 + (4.0 * c.astype(F32) + 1.5) * (1.0 / 512.0)
    step = jnp.full((1, 128), 2.0 * jnp.pi / 1024.0, F32) / middle_nu
    wide[0] = jnp.broadcast_to(comp_ref[0:1], (16, width))
    wide[1] = jnp.broadcast_to(comp_ref[1:2], (16, width))
    for ch in range(4):
        log_nu = jnp.log(jnp.full((1, width), 1.0, F32) * (base + ch / 512.0))
        bright = comp_ref[2:3] * jnp.exp(log_nu * (comp_ref[3:4] + comp_ref[4:5] * log_nu))
        wide[2 + ch] = jnp.broadcast_to(bright, (16, width))

    def block(r0, l0, channel):
        x = xb_ref[pl.ds(r0, 16)]
        y = yb_ref[pl.ds(r0, 16)]
        for j in range(width // 128):
            at = slice(128 * j, 128 * j + 128)
            turns = wide[0, :, at] * x + wide[1, :, at] * y
            r = turns - ((turns + ROUND) - ROUND)
            t = r * r
            s = r * horner(SIN_HALF, t)
            h = horner(COS_HALF, t)
            half_cos = 0.5 - s * s
            half_sin = s * h
            e = turns * step
            e2 = e * e
            s2 = e * horner(SIN_STEP, e2)
            c2 = horner(COS_STEP, e2)
            twice = c2 * c2 - 2.0
            cc, ss = half_cos * c2, half_sin * s2
            sc, cs = half_sin * c2, half_cos * s2
            cos1, cos2 = cc + ss, cc - ss
            sin1, sin2 = sc - cs, sc + cs
            cosine = (twice * cos1 - cos2, cos1, cos2, twice * cos2 - cos1)
            sine = (twice * sin1 - sin2, sin1, sin2, twice * sin2 - sin1)
            for ch in range(4):
                bright = wide[2 + ch, :, at]
                right_ref[ch, pl.ds(r0, 16), at] = (bright * cosine[ch]).astype(BF16)
                right_ref[ch, pl.ds(r0, 16), slice(width + 128 * j, width + 128 * j + 128)] = (
                    bright * sine[ch]
                ).astype(BF16)
            for first, value in ((0, cosine), (width, sine)):
                put = slice(first + 128 * j, first + 128 * j + 128)
                mine[pl.ds(r0, 16), put] = value[channel].astype(BF16)
                if l0 is not None:
                    for ch in range(4):
                        left_ref[ch, pl.ds(l0, 16), put] = value[ch].astype(BF16)
            put = slice(2 * width + 128 * j, 2 * width + 128 * j + 128)
            mine[pl.ds(r0, 16), put] = (-cosine[channel]).astype(BF16)
            if l0 is not None:
                for ch in range(4):
                    left_ref[ch, pl.ds(l0, 16), put] = (-cosine[ch]).astype(BF16)

    def run(channel):
        def own_rows(i, _):
            block(channel * quarter + 16 * i, 16 * i, channel)
            return 0

        def other_rows(first):
            def body(i, _):
                block(first + 16 * i, None, channel)
                return 0

            return body

        lax.fori_loop(0, quarter // 16, own_rows, 0)
        if channel > 0:
            lax.fori_loop(0, channel * quarter // 16, other_rows(0), 0)
        if channel < 3:
            lax.fori_loop(0, (3 - channel) * quarter // 16, other_rows((channel + 1) * quarter), 0)

    for channel in range(4):
        pl.when(k == channel)(lambda channel=channel: run(channel))

    product = lax.dot_general(
        jnp.concatenate([mine[:, : 2 * width], mine[:, width:]], axis=0),
        right_ref[k],
        NT,
        preferred_element_type=F32,
    )

    @pl.when(pl.program_id(0) == 0)
    def _():
        model_ref[...] = product

    @pl.when(pl.program_id(0) != 0)
    def _():
        model_ref[...] += product


def model_kernel(right_ref, left_ref, model_ref):
    steps = 4
    rw = right_ref.shape[2] // steps
    width = rw // 2
    lefts = []
    for q in range(steps):
        lefts.append(
            jnp.concatenate(
                [
                    left_ref[0, :, 3 * width * q : 3 * width * q + 2 * width],
                    left_ref[0, :, 3 * width * q + width : 3 * width * q + 3 * width],
                ],
                axis=0,
            )
        )
    model_ref[0] = lax.dot_general(
        jnp.concatenate(lefts, axis=1), right_ref[0], NT, preferred_element_type=F32
    )


def solve_kernel(model_ref, v0, v1, v2, v3, ok_ref, cal_ref, out_ref, a_re, a_im, b_ab, wide, part):
    k = lax.axis_index("stn")
    n = v0.shape[2]
    quarter = n // 4
    bright = cal_ref[k]
    ok = ok_ref[0:1]
    columns = lax.broadcasted_iota(jnp.int32, (8, n), 1)
    sub = lax.broadcasted_iota(jnp.int32, (8, n), 0)

    def fold(x):
        return (x[:, :128] + x[:, 128:256]) + (x[:, 256:384] + x[:, 384:])

    def set_up(s, v):
        first = lax.rem(k + 4 - s, 4) * quarter

        def body(i, _):
            local = pl.multiple_of(8 * i, 8)
            r0 = pl.multiple_of(first + 8 * i, 8)
            mr = model_ref[pl.ds(r0, 8)] + bright
            mi = model_ref[pl.ds(n + r0, 8)]
            off = columns != sub + r0
            mr = jnp.where(off, mr, 0.0)
            mi = jnp.where(off, mi, 0.0)
            vr = v[0, pl.ds(local, 8)]
            vi = v[1, pl.ds(local, 8)]
            ar = mr * vr + mi * vi
            ai = mr * vi - mi * vr
            b = mr * mr + mi * mi
            a_re[pl.ds(r0, 8)] = ar
            a_im[pl.ds(r0, 8)] = ai
            b_ab[pl.ds(r0, 8)] = b
            g = wide[0]
            part[0, pl.ds(r0, 8)] = fold(ar * g)
            part[1, pl.ds(r0, 8)] = fold(ai * g)
            part[2, pl.ds(r0, 8)] = fold(b * g)
            return 0

        lax.fori_loop(0, quarter // 8, body, 0)

    def sums():
        gr, gi, gg = wide[0], wide[1], wide[2]

        def body(i, _):
            r0 = pl.multiple_of(8 * i, 8)
            ar, ai = a_re[pl.ds(r0, 8)], a_im[pl.ds(r0, 8)]
            part[0, pl.ds(r0, 8)] = fold(ar * gr - ai * gi)
            part[1, pl.ds(r0, 8)] = fold(ar * gi + ai * gr)
            part[2, pl.ds(r0, 8)] = fold(b_ab[pl.ds(r0, 8)] * gg)
            return 0

        lax.fori_loop(0, n // 8, body, 0)

    def total(q):
        return jnp.concatenate(
            [jnp.sum(part[q, 128 * b : 128 * b + 128].T, axis=0, keepdims=True) for b in range(n // 128)], axis=1
        )

    g_re, g_im = jnp.ones((1, n), F32), jnp.zeros((1, n), F32)
    out_ref[...] = jnp.zeros_like(out_ref)
    for iteration in range(ITERS):
        wide[0] = jnp.broadcast_to(ok * g_re, (8, n))
        wide[1] = jnp.broadcast_to(ok * g_im, (8, n))
        wide[2] = jnp.broadcast_to(ok * (g_re * g_re + g_im * g_im), (8, n))
        if iteration == 0:
            for s, v in enumerate((v0, v1, v2, v3)):
                set_up(s, v)
        else:
            sums()
        below = total(2) * ok + 1e-6 + (1.0 - ok)
        new_re = total(0) * ok / below
        new_im = total(1) * ok / below
        if iteration % 2 == 1:
            new_re = 0.5 * (new_re + g_re)
            new_im = 0.5 * (new_im + g_im)
        moved = jnp.sum((new_re - g_re) ** 2 + (new_im - g_im) ** 2, axis=1, keepdims=True)
        size = jnp.sum(new_re * new_re + new_im * new_im, axis=1, keepdims=True)
        out_ref[2 + iteration : 3 + iteration] = jnp.broadcast_to(moved / (size + 1e-6), (1, n))
        g_re, g_im = new_re, new_im
    out_ref[0:1] = g_re
    out_ref[1:2] = g_im


def residual_kernel(model_ref, vis_ref, g0, g1, g2, g3, ok_ref, cal_ref, gains_ref, res_ref, change_ref, table):
    k = lax.axis_index("stn")
    ch = pl.program_id(0)
    n = vis_ref.shape[3]
    quarter = n // 4
    lanes = pl.ds(pl.multiple_of(k * quarter, 128), quarter)

    @pl.when(ch == 0)
    def _():
        for s, g in enumerate((g0, g1, g2, g3)):
            table[lax.rem(k + 4 - s, 4)] = g[...]
        lane = lax.broadcasted_iota(jnp.int32, (ITERS, 4), 1)
        history = jnp.zeros((ITERS, 4), F32)
        for q in range(4):
            gains_ref[0, q : q + 1] = table[q, 0:1, lanes]
            gains_ref[1, q : q + 1] = table[q, 1:2, lanes]
            history = jnp.where(lane == q, table[q, 2 : 2 + ITERS, 0:4], history)
        change_ref[...] = history

    bright = cal_ref[ch]

    def column(row):
        return jnp.broadcast_to(row, (128, 128)).T

    gi_re = column(table[ch, 0:1, lanes])
    gi_im = column(table[ch, 1:2, lanes])
    ui = column(ok_ref[0:1, lanes])
    columns = lax.broadcasted_iota(jnp.int32, (16, 128), 1)
    sub = lax.broadcasted_iota(jnp.int32, (16, 128), 0)
    gj_re = [jnp.broadcast_to(table[ch, 0:1, 128 * b : 128 * b + 128], (16, 128)) for b in range(4)]
    gj_im = [jnp.broadcast_to(table[ch, 1:2, 128 * b : 128 * b + 128], (16, 128)) for b in range(4)]
    uj = [jnp.broadcast_to(ok_ref[0:1, 128 * b : 128 * b + 128], (16, 128)) for b in range(4)]
    for i in range(quarter // 16):
        rows = slice(16 * i, 16 * i + 16)
        a_re, a_im, a_ok = gi_re[rows], gi_im[rows], ui[rows]
        for b in range(4):
            at = slice(128 * b, 128 * b + 128)
            off = columns + 128 * b != sub + (k * quarter + 16 * i)
            e = jnp.where(off, a_ok * uj[b], 0.0)
            p_re = a_re * gj_re[b] + a_im * gj_im[b]
            p_im = a_im * gj_re[b] - a_re * gj_im[b]
            mr = model_ref[0, rows, at] + bright
            mi = model_ref[0, slice(quarter + 16 * i, quarter + 16 * i + 16), at]
            vr = vis_ref[0, 0, rows, at].astype(F32)
            vi = vis_ref[1, 0, rows, at].astype(F32)
            res_ref[0, 0, rows, at] = (e * (vr - (p_re * mr - p_im * mi))).astype(BF16)
            res_ref[1, 0, rows, at] = (e * (vi - (p_re * mi + p_im * mr))).astype(BF16)


def per_device(visibilities, calibrator, catalog, assignment, stations, input_order, station_flags):
    rows, n = visibilities.shape[2], visibilities.shape[3]
    sources = 64 * CAP
    width = 512
    chunks = sources // width
    whole = pl.BlockSpec(memory_space=VMEM)
    smem = pl.BlockSpec(memory_space=pltpu.SMEM)
    small = pltpu.CompilerParams(vmem_limit_bytes=24 << 20)

    def shape(*dims, dtype=F32):
        return jax.ShapeDtypeStruct(dims, dtype)

    def ring(s):
        return [(i, (i + s) % 4) for i in range(4)]

    spread = pl.pallas_call(
        spread_kernel,
        out_shape=[shape(2, rows, n)] * 4,
        in_specs=[whole],
        out_specs=[whole] * 4,
        compiler_params=small,
        name="spread",
    )(visibilities)
    tiles = [spread[0]] + [lax.ppermute(spread[s], "stn", ring(s)) for s in (1, 2, 3)]

    send, xb, yb, ok = pl.pallas_call(
        route_kernel,
        out_shape=[shape(64, 1, 5 * CAP), shape(n, 128), shape(n, 128), shape(8, n)],
        in_specs=[pl.BlockSpec(memory_space=pl.ANY)] + [whole] * 4,
        out_specs=[whole] * 4,
        scratch_shapes=[VMEM((8, 128), jnp.int32), pltpu.SemaphoreType.DMA],
        compiler_params=small,
        name="route",
    )(
        assignment.reshape(-1, 128),
        catalog,
        stations,
        input_order.reshape(1, n),
        station_flags.reshape(1, n),
    )
    received = lax.all_to_all(send, "chan", 0, 0)
    components = received.reshape(64, 5, CAP).transpose(1, 0, 2).reshape(5, sources)

    right, left, model_own = pl.pallas_call(
        phasor_kernel,
        grid=(chunks,),
        out_shape=[
            shape(4, n, 2 * sources, dtype=BF16),
            shape(4, rows, 3 * sources, dtype=BF16),
            shape(2 * n, n),
        ],
        in_specs=[
            pl.BlockSpec((5, width), lambda q: (0, q)),
            pl.BlockSpec((n, 128), lambda q: (0, 0)),
            pl.BlockSpec((n, 128), lambda q: (0, 0)),
        ],
        out_specs=[
            pl.BlockSpec((4, n, 2 * width), lambda q: (0, 0, q)),
            pl.BlockSpec((4, rows, 3 * width), lambda q: (0, 0, q)),
            pl.BlockSpec((2 * n, n), lambda q: (0, 0)),
        ],
        scratch_shapes=[VMEM((6, 16, width), F32), VMEM((n, 3 * width), BF16)],
        compiler_params=pltpu.CompilerParams(vmem_limit_bytes=32 << 20),
        cost_estimate=pl.CostEstimate(flops=10 << 30, bytes_accessed=21 << 20, transcendentals=0),
        name="phasor",
    )(components, xb, yb)

    solved = pl.pallas_call(
        solve_kernel,
        out_shape=shape(8, n),
        in_specs=[whole] * 6 + [smem],
        out_specs=whole,
        scratch_shapes=[VMEM((n, n), F32)] * 3 + [VMEM((3, 8, n), F32), VMEM((3, n, 128), F32)],
        compiler_params=small,
        name="solve",
    )(model_own, *tiles, ok, calibrator)
    tables = [solved] + [lax.ppermute(solved, "stn", ring(s)) for s in (1, 2, 3)]

    model = pl.pallas_call(
        model_kernel,
        grid=(4,),
        out_shape=shape(4, 2 * rows, n),
        in_specs=[
            pl.BlockSpec((1, n, 2 * sources), lambda q: (q, 0, 0)),
            pl.BlockSpec((1, rows, 3 * sources), lambda q: (q, 0, 0)),
        ],
        out_specs=pl.BlockSpec((1, 2 * rows, n), lambda q: (q, 0, 0)),
        compiler_params=pltpu.CompilerParams(vmem_limit_bytes=32 << 20),
        cost_estimate=pl.CostEstimate(flops=5 << 30, bytes_accessed=21 << 20, transcendentals=0),
        name="model",
    )(right, left)

    row = pl.BlockSpec((8, n), lambda q: (0, 0))
    gains, residual, changes = pl.pallas_call(
        residual_kernel,
        grid=(4,),
        out_shape=[shape(2, 4, rows), shape(2, 4, rows, n, dtype=BF16), shape(ITERS, 4)],
        in_specs=[
            pl.BlockSpec((1, 2 * rows, n), lambda q: (q, 0, 0)),
            pl.BlockSpec((2, 1, rows, n), lambda q: (0, q, 0, 0)),
            row,
            row,
            row,
            row,
            row,
            smem,
        ],
        out_specs=[
            pl.BlockSpec((2, 4, rows), lambda q: (0, 0, 0)),
            pl.BlockSpec((2, 1, rows, n), lambda q: (0, q, 0, 0)),
            pl.BlockSpec((ITERS, 4), lambda q: (0, 0)),
        ],
        scratch_shapes=[VMEM((4, 8, n), F32)],
        compiler_params=small,
        name="residual",
    )(model, visibilities, *tables, ok, calibrator)
    return (gains, residual, changes)


def solution(mesh):
    placed = (P(None, "chan", "stn", None), P("chan"), P(None, "chan"), P(), P(), P(), P())
    return jax.shard_map(
        per_device,
        mesh=mesh,
        in_specs=placed,
        out_specs=(P(None, "chan", "stn"), P(None, "chan", "stn", None), P(None, "chan")),
        check_vma=False,
    )
```

```python
import jax
import jax.numpy as jnp
from jax import lax
from jax.experimental import pallas as pl
from jax.experimental.pallas import tpu as pltpu
from jax.sharding import PartitionSpec as P

ITERS = 3
CAP = 32
VMEM = pltpu.VMEM
F32 = jnp.float32
BF16 = jnp.bfloat16
NT = (((1,), (1,)), ((), ()))

SIN_HALF = (3.141582005383235, -5.167142124470761, 2.541892570102862, -0.5546189642693115)
COS_HALF = (
    0.999999953374577,
    -4.934792843915727,
    4.05841155956257,
    -1.3318775116821093,
    0.2196907395767838,
)
SIN_STEP = (1.9999932214850844, -0.33258196069982343)
COS_STEP = (1.9999999959214183, -0.9999979659209961, 0.08318303377955542)
ROUND = 12582912.0


def horner(coefficients, x):
    total = coefficients[-1]
    for c in coefficients[-2::-1]:
        total = total * x + c
    return total


def split3(x):
    high = x.astype(BF16).astype(F32)
    rest = x - high
    middle = rest.astype(BF16).astype(F32)
    return high, middle, rest - middle


def spread_kernel(vis_ref, *out_refs):
    k = lax.axis_index("stn")
    for s in range(4):
        out_refs[s][...] = vis_ref[:, lax.rem(k + s, 4)].astype(F32)


def route_kernel(assign_hbm, cat_hbm, st_hbm, order_hbm, flag_hbm, send_ref, place_ref, own, cat, st, order, flag, sem):
    c = lax.axis_index("chan")
    copies = [
        pltpu.make_async_copy(source, target, sem.at[i])
        for i, (source, target) in enumerate(
            (
                (st_hbm, st),
                (order_hbm, order),
                (flag_hbm, flag),
                (assign_hbm.at[pl.ds(pl.multiple_of(c * 8, 8), 8)], own),
                (cat_hbm, cat),
            )
        )
    ]
    for copy in copies:
        copy.start()
    n = order.shape[1]
    for copy in copies[:3]:
        copy.wait()
    hot = (lax.broadcasted_iota(jnp.int32, (n, n), 0) == order[...]).astype(F32).astype(BF16)
    high, middle, low = split3(st[...])
    rows = jnp.concatenate([high, middle, low, flag[...].astype(F32), jnp.zeros((9, n), F32)], axis=0)
    placed = jnp.dot(rows.astype(BF16), hot, preferred_element_type=F32)
    middle_nu = 1.0 + (4.0 * c.astype(F32) + 1.5) * (1.0 / 512.0)
    place_ref[...] = jnp.zeros_like(place_ref)
    place_ref[0:1] = placed[6:7]
    place_ref[1:2] = (placed[0:1] + placed[2:3] + placed[4:5]) * middle_nu
    place_ref[2:3] = (placed[1:2] + placed[3:4] + placed[5:6]) * middle_nu
    for copy in copies[3:]:
        copy.wait()
    blocks = lax.broadcasted_iota(jnp.int32, (64, 128), 0)
    hits = [(blocks == own[t : t + 1]).astype(F32) for t in range(8)]
    stacked = jnp.concatenate(hits, axis=0).astype(BF16)
    upper = lax.broadcasted_iota(jnp.int32, (128, 128), 0) <= lax.broadcasted_iota(jnp.int32, (128, 128), 1)
    running = jnp.dot(stacked, upper.astype(F32).astype(BF16), preferred_element_type=F32)
    totals = jnp.dot(stacked, jnp.ones((128, 128), BF16), preferred_element_type=F32)
    before = jnp.full((64, 128), -1.0, F32)
    slot = lax.broadcasted_iota(jnp.int32, (CAP, 128), 0).astype(F32)
    pieces = split3(cat[...])
    left, right = [], []
    for t in range(8):
        part = slice(64 * t, 64 * t + 64)
        rank = jnp.sum(hits[t] * (running[part] + before), axis=0, keepdims=True)
        before = before + totals[part]
        chosen = slot == rank
        hit = hits[t].astype(BF16)
        for piece in pieces:
            left.append(hit)
            here = piece[:, 128 * t : 128 * t + 128]
            right.append(
                jnp.concatenate([jnp.where(chosen, here[f : f + 1], 0.0) for f in range(5)], axis=0).astype(BF16)
            )
    sent = lax.dot_general(
        jnp.concatenate(left, axis=1), jnp.concatenate(right, axis=1), NT, preferred_element_type=F32
    )
    send_ref[:, 0, :] = sent


def phasor_kernel(recv_ref, place_ref, right_out, left_out, model_ref, parts, spots, rights, lefts, wides, sems):
    c = lax.axis_index("chan")
    k = lax.axis_index("stn")
    g = pl.program_id(0)
    n = model_ref.shape[1]
    quarter = n // 4
    width = 256
    tiles = width // 128
    base = 1.0 + 4.0 * c.astype(F32) * (1.0 / 512.0)
    middle_nu = 1.0 + (4.0 * c.astype(F32) + 1.5) * (1.0 / 512.0)
    step = jnp.full((8, width), 2.0 * jnp.pi / 1024.0, F32) / middle_nu

    @pl.when(g == 0)
    def _():
        got = recv_ref[:, 0, :]
        got = jnp.concatenate([got, jnp.zeros((64, 256 - got.shape[1]), F32)], axis=1)
        got = jnp.concatenate([got, jnp.zeros((64, 256), F32)], axis=0).T
        lane = lax.broadcasted_iota(jnp.int32, (16, 128), 1)
        rows = []
        for f in range(5):
            low, high = got[32 * f : 32 * f + 16], got[32 * f + 16 : 32 * f + 32]
            rows.append(jnp.where(lane < 64, low, pltpu.roll(high, 64, 1)))
        parts[0] = rows[0]
        parts[1] = rows[1]
        for ch in range(4):
            log_nu = jnp.log(jnp.full((16, 128), 1.0, F32) * (base + ch / 512.0))
            parts[2 + ch] = rows[2] * jnp.exp(log_nu * (rows[3] + rows[4] * log_nu))
        for axis in range(2):
            for b in range(n // 128):
                row = place_ref[1 + axis : 2 + axis, 128 * b : 128 * b + 128]
                spots[axis, 128 * b : 128 * b + 128] = jnp.broadcast_to(row, (128, 128)).T

    def out_copies(chunk, buffer):
        return (
            pltpu.make_async_copy(rights[buffer], right_out.at[chunk], sems.at[2 * buffer]),
            pltpu.make_async_copy(
                lefts[buffer].at[:, pl.ds(pl.multiple_of(k * quarter, quarter), quarter)],
                left_out.at[chunk],
                sems.at[2 * buffer + 1],
            ),
        )

    def phases(buffer, r0):
        right, left, wide = rights[buffer], lefts[buffer], wides[buffer]
        rows = slice(r0, r0 + 8)
        x = jnp.concatenate([spots[0, rows]] * tiles, axis=1)
        y = jnp.concatenate([spots[1, rows]] * tiles, axis=1)
        turns = wide[0] * x + wide[1] * y
        r = turns - ((turns + ROUND) - ROUND)
        t = r * r
        s = r * horner(SIN_HALF, t)
        h = horner(COS_HALF, t)
        half_cos = 0.5 - s * s
        half_sin = s * h
        e = turns * step
        e2 = e * e
        s2 = e * horner(SIN_STEP, e2)
        c2 = horner(COS_STEP, e2)
        twice = c2 * c2 - 2.0
        cc, ss = half_cos * c2, half_sin * s2
        sc, cs = half_sin * c2, half_cos * s2
        cos1, cos2 = cc + ss, cc - ss
        sin1, sin2 = sc - cs, sc + cs
        for ch, cosine, sine in (
            (1, cos1, sin1),
            (2, cos2, sin2),
            (0, twice * cos1 - cos2, twice * sin1 - sin2),
            (3, twice * cos2 - cos1, twice * sin2 - sin1),
        ):
            bright = wide[2 + ch]
            right[ch, rows, :width] = (bright * cosine).astype(BF16)
            right[ch, rows, width:] = (bright * sine).astype(BF16)
            left[ch, rows, :width] = cosine.astype(BF16)
            left[ch, rows, width:] = sine.astype(BF16)

    def product(buffer, imag, half):
        left, right = lefts[buffer], rights[buffer]
        if imag:
            lhs = jnp.concatenate([left[k, :, width:], -left[k, :, :width]], axis=1)
        else:
            lhs = left[k]
        return lax.dot_general(
            lhs, right[k, half * n // 2 : (half + 1) * n // 2], NT, preferred_element_type=F32
        )

    def accumulate(buffer, imag, half, fresh):
        out = product(buffer, imag, half)
        rows, cols = slice(imag * n, imag * n + n), slice(half * n // 2, (half + 1) * n // 2)
        if fresh is None:
            model_ref[rows, cols] += out
        else:
            model_ref[rows, cols] = jnp.where(fresh, 0.0, model_ref[rows, cols]) + out

    for sub in range(2):
        chunk = 2 * g + sub
        other = 1 - sub

        @pl.when(g > 0)
        def _():
            for copy in out_copies(chunk - 2, sub):
                copy.wait()

        for f in range(6):
            for j in range(tiles):
                row = parts[f, pl.ds(tiles * chunk + j, 1)]
                wides[sub][f, :, 128 * j : 128 * j + 128] = jnp.broadcast_to(row, (8, 128))
        for piece in range(4):
            accumulate(other, piece // 2, piece % 2, chunk <= 1)
            for i in range(quarter // 8):
                phases(sub, piece * quarter + 8 * i)
        for copy in out_copies(chunk, sub):
            copy.start()

    @pl.when(g == pl.num_programs(0) - 1)
    def _():
        for piece in range(4):
            accumulate(1, piece // 2, piece % 2, None)
        for sub in range(2):
            for copy in out_copies(2 * g + sub, sub):
                copy.wait()


def model_kernel(right_ref, left_ref, model_ref):
    chunks, half = left_ref.shape[0], left_ref.shape[3] // 2
    lefts = []
    for q in range(chunks):
        cosine, sine = left_ref[q, 0, :, :half], left_ref[q, 0, :, half:]
        lefts.append(
            jnp.concatenate(
                [jnp.concatenate([cosine, sine], axis=1), jnp.concatenate([sine, -cosine], axis=1)], axis=0
            )
        )
    model_ref[0] = lax.dot_general(
        jnp.concatenate(lefts, axis=1),
        jnp.concatenate([right_ref[q, 0] for q in range(chunks)], axis=1),
        NT,
        preferred_element_type=F32,
    )


def solve_kernel(model_ref, v0, v1, v2, v3, ok_ref, cal_ref, out_ref, a_re, a_im, b_ab, wide, part):
    k = lax.axis_index("stn")
    n = v0.shape[2]
    quarter = n // 4
    bright = cal_ref[k]
    ok = ok_ref[0:1]
    columns = lax.broadcasted_iota(jnp.int32, (8, n), 1)
    sub = lax.broadcasted_iota(jnp.int32, (8, n), 0)

    def fold(x):
        return (x[:, :128] + x[:, 128:256]) + (x[:, 256:384] + x[:, 384:])

    def set_up(s, v):
        first = lax.rem(k + 4 - s, 4) * quarter

        def body(i, _):
            local = pl.multiple_of(8 * i, 8)
            r0 = pl.multiple_of(first + 8 * i, 8)
            mr = model_ref[pl.ds(r0, 8)] + bright
            mi = model_ref[pl.ds(n + r0, 8)]
            off = columns != sub + r0
            mr = jnp.where(off, mr, 0.0)
            mi = jnp.where(off, mi, 0.0)
            vr = v[0, pl.ds(local, 8)]
            vi = v[1, pl.ds(local, 8)]
            ar = mr * vr + mi * vi
            ai = mr * vi - mi * vr
            b = mr * mr + mi * mi
            a_re[pl.ds(r0, 8)] = ar
            a_im[pl.ds(r0, 8)] = ai
            b_ab[pl.ds(r0, 8)] = b
            g = wide[0]
            part[0, pl.ds(r0, 8)] = fold(ar * g)
            part[1, pl.ds(r0, 8)] = fold(ai * g)
            part[2, pl.ds(r0, 8)] = fold(b * g)
            return 0

        lax.fori_loop(0, quarter // 8, body, 0)

    def sums():
        gr, gi, gg = wide[0], wide[1], wide[2]

        def body(i, _):
            r0 = pl.multiple_of(8 * i, 8)
            ar, ai = a_re[pl.ds(r0, 8)], a_im[pl.ds(r0, 8)]
            part[0, pl.ds(r0, 8)] = fold(ar * gr - ai * gi)
            part[1, pl.ds(r0, 8)] = fold(ar * gi + ai * gr)
            part[2, pl.ds(r0, 8)] = fold(b_ab[pl.ds(r0, 8)] * gg)
            return 0

        lax.fori_loop(0, n // 8, body, 0)

    def total(q):
        return jnp.concatenate(
            [jnp.sum(part[q, 128 * b : 128 * b + 128].T, axis=0, keepdims=True) for b in range(n // 128)], axis=1
        )

    g_re, g_im = jnp.ones((1, n), F32), jnp.zeros((1, n), F32)
    out_ref[...] = jnp.zeros_like(out_ref)
    for iteration in range(ITERS):
        wide[0] = jnp.broadcast_to(ok * g_re, (8, n))
        wide[1] = jnp.broadcast_to(ok * g_im, (8, n))
        wide[2] = jnp.broadcast_to(ok * (g_re * g_re + g_im * g_im), (8, n))
        if iteration == 0:
            for s, v in enumerate((v0, v1, v2, v3)):
                set_up(s, v)
        else:
            sums()
        below = total(2) * ok + 1e-6 + (1.0 - ok)
        new_re = total(0) * ok / below
        new_im = total(1) * ok / below
        if iteration % 2 == 1:
            new_re = 0.5 * (new_re + g_re)
            new_im = 0.5 * (new_im + g_im)
        moved = jnp.sum((new_re - g_re) ** 2 + (new_im - g_im) ** 2, axis=1, keepdims=True)
        size = jnp.sum(new_re * new_re + new_im * new_im, axis=1, keepdims=True)
        out_ref[2 + iteration : 3 + iteration] = jnp.broadcast_to(moved / (size + 1e-6), (1, n))
        g_re, g_im = new_re, new_im
    out_ref[0:1] = g_re
    out_ref[1:2] = g_im


def residual_kernel(model_ref, vis_ref, g0, g1, g2, g3, ok_ref, cal_ref, gains_ref, res_ref, change_ref, table):
    k = lax.axis_index("stn")
    ch = pl.program_id(0)
    n = vis_ref.shape[3]
    quarter = n // 4
    lanes = pl.ds(pl.multiple_of(k * quarter, 128), quarter)

    @pl.when(ch == 0)
    def _():
        for s, g in enumerate((g0, g1, g2, g3)):
            table[lax.rem(k + 4 - s, 4)] = g[...]
        lane = lax.broadcasted_iota(jnp.int32, (ITERS, 4), 1)
        history = jnp.zeros((ITERS, 4), F32)
        for q in range(4):
            gains_ref[0, q : q + 1] = table[q, 0:1, lanes]
            gains_ref[1, q : q + 1] = table[q, 1:2, lanes]
            history = jnp.where(lane == q, table[q, 2 : 2 + ITERS, 0:4], history)
        change_ref[...] = history

    bright = cal_ref[ch]

    def column(row):
        return jnp.broadcast_to(row, (128, 128)).T

    gi_re = column(table[ch, 0:1, lanes])
    gi_im = column(table[ch, 1:2, lanes])
    ui = column(ok_ref[0:1, lanes])
    columns = lax.broadcasted_iota(jnp.int32, (16, 128), 1)
    sub = lax.broadcasted_iota(jnp.int32, (16, 128), 0)
    gj_re = [jnp.broadcast_to(table[ch, 0:1, 128 * b : 128 * b + 128], (16, 128)) for b in range(4)]
    gj_im = [jnp.broadcast_to(table[ch, 1:2, 128 * b : 128 * b + 128], (16, 128)) for b in range(4)]
    uj = [jnp.broadcast_to(ok_ref[0:1, 128 * b : 128 * b + 128], (16, 128)) for b in range(4)]
    for i in range(quarter // 16):
        rows = slice(16 * i, 16 * i + 16)
        a_re, a_im, a_ok = gi_re[rows], gi_im[rows], ui[rows]
        for b in range(4):
            at = slice(128 * b, 128 * b + 128)
            off = columns + 128 * b != sub + (k * quarter + 16 * i)
            e = jnp.where(off, a_ok * uj[b], 0.0)
            p_re = a_re * gj_re[b] + a_im * gj_im[b]
            p_im = a_im * gj_re[b] - a_re * gj_im[b]
            mr = model_ref[0, rows, at] + bright
            mi = model_ref[0, slice(quarter + 16 * i, quarter + 16 * i + 16), at]
            vr = vis_ref[0, 0, rows, at].astype(F32)
            vi = vis_ref[1, 0, rows, at].astype(F32)
            res_ref[0, 0, rows, at] = (e * (vr - (p_re * mr - p_im * mi))).astype(BF16)
            res_ref[1, 0, rows, at] = (e * (vi - (p_re * mi + p_im * mr))).astype(BF16)


def per_device(visibilities, calibrator, catalog, assignment, stations, input_order, station_flags):
    rows, n = visibilities.shape[2], visibilities.shape[3]
    sources = 64 * CAP
    chunks = sources // 256
    whole = pl.BlockSpec(memory_space=VMEM)
    smem = pl.BlockSpec(memory_space=pltpu.SMEM)
    hbm = pl.BlockSpec(memory_space=pltpu.HBM)
    small = pltpu.CompilerParams(vmem_limit_bytes=24 << 20)

    def shape(*dims, dtype=F32):
        return jax.ShapeDtypeStruct(dims, dtype)

    def ring(s):
        return [(i, (i + s) % 4) for i in range(4)]

    send, place = pl.pallas_call(
        route_kernel,
        out_shape=[shape(64, 1, 5 * CAP), shape(8, n)],
        in_specs=[hbm] * 5,
        out_specs=[whole] * 2,
        scratch_shapes=[
            VMEM((8, 128), jnp.int32),
            VMEM(catalog.shape, F32),
            VMEM(stations.shape, F32),
            VMEM((1, n), jnp.int32),
            VMEM((1, n), jnp.int32),
            pltpu.SemaphoreType.DMA((5,)),
        ],
        compiler_params=small,
        name="route",
    )(
        assignment.reshape(-1, 128),
        catalog,
        stations,
        input_order.reshape(1, n),
        station_flags.reshape(1, n),
    )
    received = lax.all_to_all(send, "chan", 0, 0)

    spread = pl.pallas_call(
        spread_kernel,
        out_shape=[shape(2, rows, n)] * 4,
        in_specs=[whole],
        out_specs=[whole] * 4,
        compiler_params=small,
        name="spread",
    )(visibilities)
    tiles = [spread[0]] + [lax.ppermute(spread[s], "stn", ring(s)) for s in (1, 2, 3)]

    right, left, model_own = pl.pallas_call(
        phasor_kernel,
        grid=(chunks // 2,),
        out_shape=[
            shape(chunks, 4, n, 512, dtype=BF16),
            shape(chunks, 4, rows, 512, dtype=BF16),
            shape(2 * n, n),
        ],
        in_specs=[
            pl.BlockSpec((64, 1, 5 * CAP), lambda g: (0, 0, 0)),
            pl.BlockSpec((8, n), lambda g: (0, 0)),
        ],
        out_specs=[hbm, hbm, pl.BlockSpec((2 * n, n), lambda g: (0, 0))],
        scratch_shapes=[
            VMEM((6, 16, 128), F32),
            VMEM((2, n, 128), F32),
            [VMEM((4, n, 512), BF16)] * 2,
            [VMEM((4, n, 512), BF16)] * 2,
            [VMEM((6, 8, 256), F32)] * 2,
            pltpu.SemaphoreType.DMA((4,)),
        ],
        compiler_params=pltpu.CompilerParams(vmem_limit_bytes=32 << 20),
        cost_estimate=pl.CostEstimate(flops=10 << 30, bytes_accessed=21 << 20, transcendentals=0),
        name="phasor",
    )(received, place)

    solved = pl.pallas_call(
        solve_kernel,
        out_shape=shape(8, n),
        in_specs=[whole] * 6 + [smem],
        out_specs=whole,
        scratch_shapes=[VMEM((n, n), F32)] * 3 + [VMEM((3, 8, n), F32), VMEM((3, n, 128), F32)],
        compiler_params=small,
        name="solve",
    )(model_own, *tiles, place, calibrator)
    tables = [solved] + [lax.ppermute(solved, "stn", ring(s)) for s in (1, 2, 3)]

    model = pl.pallas_call(
        model_kernel,
        grid=(4,),
        out_shape=shape(4, 2 * rows, n),
        in_specs=[
            pl.BlockSpec((chunks, 1, n, 512), lambda q: (0, q, 0, 0)),
            pl.BlockSpec((chunks, 1, rows, 512), lambda q: (0, q, 0, 0)),
        ],
        out_specs=pl.BlockSpec((1, 2 * rows, n), lambda q: (q, 0, 0)),
        compiler_params=pltpu.CompilerParams(vmem_limit_bytes=32 << 20),
        cost_estimate=pl.CostEstimate(flops=5 << 30, bytes_accessed=21 << 20, transcendentals=0),
        name="model",
    )(right, left)

    row = pl.BlockSpec((8, n), lambda q: (0, 0))
    gains, residual, changes = pl.pallas_call(
        residual_kernel,
        grid=(4,),
        out_shape=[shape(2, 4, rows), shape(2, 4, rows, n, dtype=BF16), shape(ITERS, 4)],
        in_specs=[
            pl.BlockSpec((1, 2 * rows, n), lambda q: (q, 0, 0)),
            pl.BlockSpec((2, 1, rows, n), lambda q: (0, q, 0, 0)),
            row,
            row,
            row,
            row,
            row,
            smem,
        ],
        out_specs=[
            pl.BlockSpec((2, 4, rows), lambda q: (0, 0, 0)),
            pl.BlockSpec((2, 1, rows, n), lambda q: (0, q, 0, 0)),
            pl.BlockSpec((ITERS, 4), lambda q: (0, 0)),
        ],
        scratch_shapes=[VMEM((4, 8, n), F32)],
        compiler_params=small,
        name="residual",
    )(model, visibilities, *tables, place, calibrator)
    return (gains, residual, changes)


def solution(mesh):
    placed = (P(None, "chan", "stn", None), P("chan"), P(None, "chan"), P(), P(), P(), P())
    return jax.shard_map(
        per_device,
        mesh=mesh,
        in_specs=placed,
        out_specs=(P(None, "chan", "stn"), P(None, "chan", "stn", None), P(None, "chan")),
        check_vma=False,
    )
```

```python
import jax
import jax.numpy as jnp
from jax import lax
from jax.experimental import pallas as pl
from jax.experimental.pallas import tpu as pltpu
from jax.sharding import PartitionSpec as P


ITERS = 3
CAP = 32
VMEM = pltpu.VMEM
F32 = jnp.float32
BF16 = jnp.bfloat16
NT = (((1,), (1,)), ((), ()))

SIN_HALF = (3.141582005383235, -5.167142124470761, 2.541892570102862, -0.5546189642693115)
COS_HALF = (
    0.999999953374577,
    -4.934792843915727,
    4.05841155956257,
    -1.3318775116821093,
    0.2196907395767838,
)
SIN_STEP = (1.9999932214850844, -0.33258196069982343)
COS_STEP = (1.9999999959214183, -0.9999979659209961, 0.08318303377955542)
ROUND = 12582912.0


def horner(coefficients, x):
    total = coefficients[-1]
    for c in coefficients[-2::-1]:
        total = total * x + c
    return total


def split3(x):
    high = x.astype(BF16).astype(F32)
    rest = x - high
    middle = rest.astype(BF16).astype(F32)
    return high, middle, rest - middle


def front_kernel(
    vis_hbm, assign_hbm, cat_hbm, st_hbm, order_hbm, flag_hbm, cal_hbm, *refs
):
    send_ref, place_ref, tiles = refs[0], refs[1], refs[2:6]
    vis, own, cat, st, order, flag, cal, sem = refs[6:]
    c = lax.axis_index("chan")
    k = lax.axis_index("stn")
    copies = [
        pltpu.make_async_copy(source, target, sem.at[i])
        for i, (source, target) in enumerate(
            (
                (st_hbm, st),
                (order_hbm, order),
                (flag_hbm, flag),
                (assign_hbm.at[pl.ds(pl.multiple_of(c * 8, 8), 8)], own),
                (cat_hbm, cat),
                (vis_hbm, vis),
                (cal_hbm, cal),
            )
        )
    ]
    for copy in copies:
        copy.start()
    n = order.shape[1]
    for copy in copies[:3] + copies[6:]:
        copy.wait()
    hot = (lax.broadcasted_iota(jnp.int32, (n, n), 0) == order[...]).astype(F32).astype(BF16)
    high, middle, low = split3(st[...])
    rows = jnp.concatenate([high, middle, low, flag[...].astype(F32), jnp.zeros((9, n), F32)], axis=0)
    placed = jnp.dot(rows.astype(BF16), hot, preferred_element_type=F32)
    middle_nu = 1.0 + (4.0 * c.astype(F32) + 1.5) * (1.0 / 512.0)
    place_ref[...] = jnp.zeros_like(place_ref)
    place_ref[0:1] = placed[6:7]
    for ch in range(4):
        place_ref[4 + ch : 5 + ch] = jnp.broadcast_to(cal[:, ch : ch + 1], (1, n))
    place_ref[1:2] = (placed[0:1] + placed[2:3] + placed[4:5]) * middle_nu
    place_ref[2:3] = (placed[1:2] + placed[3:4] + placed[5:6]) * middle_nu
    for copy in copies[3:5]:
        copy.wait()
    blocks = lax.broadcasted_iota(jnp.int32, (64, 128), 0)
    hits = [(blocks == own[t : t + 1]).astype(F32) for t in range(8)]
    stacked = jnp.concatenate(hits, axis=0).astype(BF16)
    upper = lax.broadcasted_iota(jnp.int32, (128, 128), 0) <= lax.broadcasted_iota(jnp.int32, (128, 128), 1)
    running = jnp.dot(stacked, upper.astype(F32).astype(BF16), preferred_element_type=F32)
    totals = jnp.dot(stacked, jnp.ones((128, 128), BF16), preferred_element_type=F32)
    before = jnp.full((64, 128), -1.0, F32)
    slot = lax.broadcasted_iota(jnp.int32, (CAP, 128), 0).astype(F32)
    pieces = split3(cat[...])
    left, right = [], []
    for t in range(8):
        part = slice(64 * t, 64 * t + 64)
        rank = jnp.sum(hits[t] * (running[part] + before), axis=0, keepdims=True)
        before = before + totals[part]
        chosen = slot == rank
        hit = hits[t].astype(BF16)
        for piece in pieces:
            left.append(hit)
            here = piece[:, 128 * t : 128 * t + 128]
            right.append(
                jnp.concatenate([jnp.where(chosen, here[f : f + 1], 0.0) for f in range(5)], axis=0).astype(BF16)
            )
    sent = lax.dot_general(
        jnp.concatenate(left, axis=1), jnp.concatenate(right, axis=1), NT, preferred_element_type=F32
    )
    send_ref[:, 0, :] = sent
    copies[5].wait()
    for s in range(4):
        tiles[s][...] = vis[:, lax.rem(k + s, 4)].astype(F32)


def spots_kernel(place_ref, spots_ref, out_ref):
    for axis in range(2):
        for b in range(spots_ref.shape[1] // 128):
            row = place_ref[1 + axis : 2 + axis, 128 * b : 128 * b + 128]
            spots_ref[axis, 128 * b : 128 * b + 128] = jnp.broadcast_to(row, (128, 128)).T
    out_ref[...] = place_ref[...]


def phasor_kernel(recv_ref, spots, place_ref, right_out, left_out, model_ref, parts, bright_rows, rights, lefts, wides, sems):
    c = lax.axis_index("chan")
    k = lax.axis_index("stn")
    n = model_ref.shape[1]
    quarter = n // 4
    width = 256
    pairs = right_out.shape[0] // 2
    tiles = width // 128
    base = 1.0 + 4.0 * c.astype(F32) * (1.0 / 512.0)
    middle_nu = 1.0 + (4.0 * c.astype(F32) + 1.5) * (1.0 / 512.0)
    step = jnp.full((8, width), 2.0 * jnp.pi / 1024.0, F32) / middle_nu

    got = recv_ref[:, 0, :]
    got = jnp.concatenate([got, jnp.zeros((64, 256 - got.shape[1]), F32)], axis=1)
    got = jnp.concatenate([got, jnp.zeros((64, 256), F32)], axis=0).T
    lane = lax.broadcasted_iota(jnp.int32, (16, 128), 1)
    rows = []
    for f in range(5):
        low, high = got[32 * f : 32 * f + 16], got[32 * f + 16 : 32 * f + 32]
        rows.append(jnp.where(lane < 64, low, pltpu.roll(high, 64, 1)))
    parts[0] = rows[0]
    parts[1] = rows[1]
    for ch in range(4):
        log_nu = jnp.log(jnp.full((16, 128), 1.0, F32) * (base + ch / 512.0))
        parts[2 + ch] = rows[2] * jnp.exp(log_nu * (rows[3] + rows[4] * log_nu))

    def out_copies(chunk, buffer):
        return (
            pltpu.make_async_copy(rights[buffer], right_out.at[chunk], sems.at[2 * buffer]),
            pltpu.make_async_copy(
                lefts[buffer].at[:, pl.ds(pl.multiple_of(k * quarter, quarter), quarter)],
                left_out.at[chunk],
                sems.at[2 * buffer + 1],
            ),
        )

    def phases(buffer, r0):
        right, left, wide = rights[buffer], lefts[buffer], wides[buffer]
        rows = slice(r0, r0 + 8)
        x = jnp.concatenate([spots[0, rows]] * tiles, axis=1)
        y = jnp.concatenate([spots[1, rows]] * tiles, axis=1)
        turns = wide[0] * x + wide[1] * y
        r = turns - ((turns + ROUND) - ROUND)
        t = r * r
        s = r * horner(SIN_HALF, t)
        h = horner(COS_HALF, t)
        half_cos = 0.5 - s * s
        half_sin = s * h
        e = turns * step
        e2 = e * e
        s2 = e * horner(SIN_STEP, e2)
        c2 = horner(COS_STEP, e2)
        twice = c2 * c2 - 2.0
        cc, ss = half_cos * c2, half_sin * s2
        sc, cs = half_sin * c2, half_cos * s2
        cos1, cos2 = cc + ss, cc - ss
        sin1, sin2 = sc - cs, sc + cs
        for ch, cosine, sine in (
            (1, cos1, sin1),
            (2, cos2, sin2),
            (0, twice * cos1 - cos2, twice * sin1 - sin2),
            (3, twice * cos2 - cos1, twice * sin2 - sin1),
        ):
            bright = wide[2 + ch]
            right[ch, rows, :width] = (bright * cosine).astype(BF16)
            right[ch, rows, width:] = (bright * sine).astype(BF16)
            left[ch, rows, :width] = cosine.astype(BF16)
            left[ch, rows, width:] = sine.astype(BF16)

    for f in range(2):
        (lefts, rights)[f][1][k] = jnp.zeros((n, 2 * width), BF16)

    def chunks(*totals):
        def matmul(other, turn, block):
            left, right = lefts[other], rights[other]
            columns = slice(turn * width, turn * width + width)
            if block == 0:
                for half in range(2):
                    pltpu.matmul_push_rhs(
                        right[k, half * width : half * width + width, columns], turn, half, transpose=True
                    )
            rows = slice(128 * (block % 4), 128 * (block % 4) + 128)
            if block < 4:
                lhs = left[k, rows, columns]
            else:
                lhs = left[k, rows, (1 - turn) * width : (2 - turn) * width]
                if turn == 1:
                    lhs = -lhs
            for half in range(2):
                pltpu.matmul_acc_lhs(totals[8 * half + block], lhs, turn if block == 0 else None)

        def pair(g, _):
            for sub in range(2):
                chunk = 2 * g + sub

                @pl.when(g > 0)
                def _():
                    for copy in out_copies(chunk - 2, sub):
                        copy.wait()

                for f in range(6):
                    for j in range(tiles):
                        row = parts[f, pl.ds(tiles * chunk + j, 1)]
                        wides[sub][f, :, 128 * j : 128 * j + 128] = jnp.broadcast_to(row, (8, 128))
                for turn in range(2):
                    for block in range(8):

                        def body(sub=sub, turn=turn, block=block):
                            matmul(1 - sub, turn, block)
                            for i in range(4):
                                phases(sub, 32 * (8 * turn + block) + 8 * i)

                        pl.when(g >= 0)(body)
                for copy in out_copies(chunk, sub):
                    copy.start()
            return 0

        lax.fori_loop(0, pairs, pair, 0)
        for turn in range(2):
            for block in range(8):
                matmul(1, turn, block)
        for sub in range(2):
            for copy in out_copies(2 * pairs - 2 + sub, sub):
                copy.wait()
        bright_rows[0:4] = place_ref[4:8, :128]
        bright = bright_rows[pl.ds(k, 1)]
        bright = jnp.concatenate([bright, bright], axis=1)
        off = lax.broadcasted_iota(jnp.int32, (128, 128), 0) != lax.broadcasted_iota(jnp.int32, (128, 128), 1)
        for block in range(8):
            rows = slice(128 * block, 128 * block + 128)
            for half in range(2):
                total = pltpu.matmul_pop(totals[8 * half + block])
                if block < 4:
                    total = total + bright
                for j in range(2):
                    part = total[:, 128 * j : 128 * j + 128]
                    column = 2 * half + j
                    if column == block % 4:
                        part = jnp.where(off, part, 0.0)
                    model_ref[rows, 128 * column : 128 * column + 128] = part

    pl.run_scoped(chunks, *[pltpu.ACC(half)((128, 256), F32) for half in range(2) for _ in range(8)])


def model_kernel(right_ref, left_ref, model_ref):
    chunks, half = left_ref.shape[0], left_ref.shape[3] // 2

    def channel(ch, _):
        lefts = []
        for q in range(chunks):
            left = left_ref[q, ch]
            cosine, sine = left[:, :half], left[:, half:]
            lefts.append(jnp.concatenate([left, jnp.concatenate([sine, -cosine], axis=1)], axis=0))
        model_ref[ch] = lax.dot_general(
            jnp.concatenate(lefts, axis=1),
            jnp.concatenate([right_ref[q, ch] for q in range(chunks)], axis=1),
            NT,
            preferred_element_type=F32,
        )
        return 0

    lax.fori_loop(0, 4, channel, 0)


def solve_kernel(model_ref, v0, v1, v2, v3, ok_ref, out_ref, a_re, a_im, b_ab, wide, part):
    k = lax.axis_index("stn")
    n = v0.shape[2]
    quarter = n // 4
    ok = ok_ref[0:1]

    def fold(x):
        return (x[:, :128] + x[:, 128:256]) + (x[:, 256:384] + x[:, 384:])

    def set_up(s, v):
        first = lax.rem(k + 4 - s, 4) * quarter

        def body(i, _):
            local = pl.multiple_of(8 * i, 8)
            r0 = pl.multiple_of(first + 8 * i, 8)
            mr = model_ref[pl.ds(r0, 8)]
            mi = model_ref[pl.ds(n + r0, 8)]
            vr = v[0, pl.ds(local, 8)]
            vi = v[1, pl.ds(local, 8)]
            ar = mr * vr + mi * vi
            ai = mr * vi - mi * vr
            b = mr * mr + mi * mi
            a_re[pl.ds(r0, 8)] = ar
            a_im[pl.ds(r0, 8)] = ai
            b_ab[pl.ds(r0, 8)] = b
            g = wide[0]
            part[0, pl.ds(r0, 8)] = fold(ar * g)
            part[1, pl.ds(r0, 8)] = fold(ai * g)
            part[2, pl.ds(r0, 8)] = fold(b * g)
            return 0

        lax.fori_loop(0, quarter // 8, body, 0, unroll=4)

    def sums():
        gr, gi, gg = wide[0], wide[1], wide[2]

        def body(i, _):
            r0 = pl.multiple_of(8 * i, 8)
            ar, ai = a_re[pl.ds(r0, 8)], a_im[pl.ds(r0, 8)]
            part[0, pl.ds(r0, 8)] = fold(ar * gr - ai * gi)
            part[1, pl.ds(r0, 8)] = fold(ar * gi + ai * gr)
            part[2, pl.ds(r0, 8)] = fold(b_ab[pl.ds(r0, 8)] * gg)
            return 0

        lax.fori_loop(0, n // 8, body, 0, unroll=4)

    def total(q):
        return jnp.concatenate(
            [jnp.sum(part[q, 128 * b : 128 * b + 128].T, axis=0, keepdims=True) for b in range(n // 128)], axis=1
        )

    g_re, g_im = jnp.ones((1, n), F32), jnp.zeros((1, n), F32)
    out_ref[...] = jnp.zeros_like(out_ref)
    for iteration in range(ITERS):
        wide[0] = jnp.broadcast_to(ok * g_re, (8, n))
        wide[1] = jnp.broadcast_to(ok * g_im, (8, n))
        wide[2] = jnp.broadcast_to(ok * (g_re * g_re + g_im * g_im), (8, n))
        if iteration == 0:
            for s, v in enumerate((v0, v1, v2, v3)):
                set_up(s, v)
        else:
            sums()
        below = total(2) * ok + 1e-6 + (1.0 - ok)
        new_re = total(0) * ok / below
        new_im = total(1) * ok / below
        if iteration % 2 == 1:
            new_re = 0.5 * (new_re + g_re)
            new_im = 0.5 * (new_im + g_im)
        moved = jnp.sum((new_re - g_re) ** 2 + (new_im - g_im) ** 2, axis=1, keepdims=True)
        size = jnp.sum(new_re * new_re + new_im * new_im, axis=1, keepdims=True)
        out_ref[2 + iteration : 3 + iteration] = jnp.broadcast_to(moved / (size + 1e-6), (1, n))
        g_re, g_im = new_re, new_im
    out_ref[0:1] = g_re
    out_ref[1:2] = g_im


def residual_kernel(model_ref, vis_ref, g0, g1, g2, g3, ok_ref, gains_ref, res_ref, change_ref, table, wide):
    k = lax.axis_index("stn")
    ch = pl.program_id(0)
    n = vis_ref.shape[3]
    quarter = n // 4
    lanes = pl.ds(pl.multiple_of(k * quarter, 128), quarter)

    @pl.when(ch == 0)
    def _():
        wide[0:4] = ok_ref[4:8, :128]
        for s, g in enumerate((g0, g1, g2, g3)):
            table[lax.rem(k + 4 - s, 4)] = g[...]
        lane = lax.broadcasted_iota(jnp.int32, (ITERS, 4), 1)
        history = jnp.zeros((ITERS, 4), F32)
        for q in range(4):
            gains_ref[0, q : q + 1] = table[q, 0:1, lanes]
            gains_ref[1, q : q + 1] = table[q, 1:2, lanes]
            history = jnp.where(lane == q, table[q, 2 : 2 + ITERS, 0:4], history)
        change_ref[...] = history

    bright = wide[pl.ds(ch, 1)]

    def column(row):
        return jnp.broadcast_to(row, (128, 128)).T

    gi_re = column(table[ch, 0:1, lanes])
    gi_im = column(table[ch, 1:2, lanes])
    ui = column(ok_ref[0:1, lanes])
    columns = lax.broadcasted_iota(jnp.int32, (16, 128), 1)
    sub = lax.broadcasted_iota(jnp.int32, (16, 128), 0)
    gj_re = [jnp.broadcast_to(table[ch, 0:1, 128 * b : 128 * b + 128], (16, 128)) for b in range(4)]
    gj_im = [jnp.broadcast_to(table[ch, 1:2, 128 * b : 128 * b + 128], (16, 128)) for b in range(4)]
    uj = [jnp.broadcast_to(ok_ref[0:1, 128 * b : 128 * b + 128], (16, 128)) for b in range(4)]
    for i in range(quarter // 16):
        rows = slice(16 * i, 16 * i + 16)
        a_re, a_im, a_ok = gi_re[rows], gi_im[rows], ui[rows]
        for b in range(4):
            at = slice(128 * b, 128 * b + 128)
            off = columns + 128 * b != sub + (k * quarter + 16 * i)
            e = jnp.where(off, a_ok * uj[b], 0.0)
            p_re = a_re * gj_re[b] + a_im * gj_im[b]
            p_im = a_im * gj_re[b] - a_re * gj_im[b]
            mr = model_ref[ch, rows, at] + bright
            mi = model_ref[ch, slice(quarter + 16 * i, quarter + 16 * i + 16), at]
            vr = vis_ref[0, ch, rows, at].astype(F32)
            vi = vis_ref[1, ch, rows, at].astype(F32)
            res_ref[0, 0, rows, at] = (e * (vr - (p_re * mr - p_im * mi))).astype(BF16)
            res_ref[1, 0, rows, at] = (e * (vi - (p_re * mi + p_im * mr))).astype(BF16)


def per_device(visibilities, calibrator, catalog, assignment, stations, input_order, station_flags):
    rows, n = visibilities.shape[2], visibilities.shape[3]
    sources = 64 * CAP
    chunks = sources // 256
    whole = pl.BlockSpec(memory_space=VMEM)
    hbm = pl.BlockSpec(memory_space=pltpu.HBM)
    small = pltpu.CompilerParams(vmem_limit_bytes=8 << 20)

    def shape(*dims, dtype=F32):
        return jax.ShapeDtypeStruct(dims, dtype)

    def ring(s):
        return [(i, (i + s) % 4) for i in range(4)]

    send, place, *own = pl.pallas_call(
        front_kernel,
        out_shape=[shape(64, 1, 5 * CAP), shape(8, n)] + [shape(2, rows, n)] * 4,
        in_specs=[hbm] * 7,
        out_specs=[whole] * 6,
        scratch_shapes=[
            VMEM(visibilities.shape, BF16),
            VMEM((8, 128), jnp.int32),
            VMEM(catalog.shape, F32),
            VMEM(stations.shape, F32),
            VMEM((1, n), jnp.int32),
            VMEM((1, n), jnp.int32),
            VMEM((1, 4), F32),
            pltpu.SemaphoreType.DMA((7,)),
        ],
        name="front",
    )(
        visibilities,
        assignment.reshape(-1, 128),
        catalog,
        stations,
        input_order.reshape(1, n),
        station_flags.reshape(1, n),
        calibrator.reshape(1, 4),
    )

    def turn(s):
        return lax.ppermute(own[s], "stn", ring(s))

    received = lax.all_to_all(send, "chan", 0, 0)
    tiles = [own[0], turn(1), turn(2), turn(3)]
    spots, place = pl.pallas_call(
        spots_kernel,
        out_shape=[shape(2, n, 128), shape(8, n)],
        in_specs=[whole],
        out_specs=[whole] * 2,
        compiler_params=small,
        name="spots",
    )(place)

    right, left, model_own = pl.pallas_call(
        phasor_kernel,
        out_shape=[
            shape(chunks, 4, n, 512, dtype=BF16),
            shape(chunks, 4, rows, 512, dtype=BF16),
            shape(2 * n, n),
        ],
        in_specs=[whole] * 3,
        out_specs=[hbm, hbm, whole],
        scratch_shapes=[
            VMEM((6, 16, 128), F32),
            VMEM((8, 128), F32),
            [VMEM((4, n, 512), BF16)] * 2,
            [VMEM((4, n, 512), BF16)] * 2,
            [VMEM((6, 8, 256), F32)] * 2,
            pltpu.SemaphoreType.DMA((4,)),
        ],
        compiler_params=pltpu.CompilerParams(vmem_limit_bytes=14 << 20),
        cost_estimate=pl.CostEstimate(flops=10 << 30, bytes_accessed=21 << 20, transcendentals=0),
        name="phasor",
    )(received, spots, place)

    solved = pl.pallas_call(
        solve_kernel,
        out_shape=shape(8, n),
        in_specs=[whole] * 6,
        out_specs=whole,
        scratch_shapes=[VMEM((n, n), F32)] * 3 + [VMEM((3, 8, n), F32), VMEM((3, n, 128), F32)],
        compiler_params=small,
        name="solve",
    )(model_own, *tiles, place)
    tables = [solved] + [lax.ppermute(solved, "stn", ring(s)) for s in (1, 2, 3)]

    model = pl.pallas_call(
        model_kernel,
        out_shape=shape(4, 2 * rows, n),
        in_specs=[whole] * 2,
        out_specs=whole,
        compiler_params=small,
        cost_estimate=pl.CostEstimate(flops=5 << 30, bytes_accessed=21 << 20, transcendentals=0),
        name="model",
    )(right, left)

    gains, residual, changes = pl.pallas_call(
        residual_kernel,
        grid=(4,),
        out_shape=[shape(2, 4, rows), shape(2, 4, rows, n, dtype=BF16), shape(ITERS, 4)],
        in_specs=[whole] * 7,
        out_specs=[
            pl.BlockSpec((2, 4, rows), lambda q: (0, 0, 0)),
            pl.BlockSpec((2, 1, rows, n), lambda q: (0, q, 0, 0)),
            pl.BlockSpec((ITERS, 4), lambda q: (0, 0)),
        ],
        scratch_shapes=[VMEM((4, 8, n), F32), VMEM((8, 128), F32)],
        compiler_params=small,
        name="residual",
    )(model, visibilities, *tables, place)
    return (gains, residual, changes)


def solution(mesh):
    placed = (P(None, "chan", "stn", None), P("chan"), P(None, "chan"), P(), P(), P(), P())

    return jax.shard_map(
        per_device,
        mesh=mesh,
        in_specs=placed,
        out_specs=(P(None, "chan", "stn"), P(None, "chan", "stn", None), P(None, "chan")),
        check_vma=False,
    )
```

```python
import jax
import jax.numpy as jnp
from jax import lax
from jax.experimental import pallas as pl
from jax.experimental.pallas import tpu as pltpu
from jax.sharding import PartitionSpec as P


ITERS = 3
CAP = 32
VMEM = pltpu.VMEM
F32 = jnp.float32
BF16 = jnp.bfloat16
NT = (((1,), (1,)), ((), ()))

SIN_HALF = (3.141582005383235, -5.167142124470761, 2.541892570102862, -0.5546189642693115)
COS_HALF = (0.9999932847330446, -4.93393699910271, 4.041270253370243, -1.2220835776975139)
SIN_STEP = (1.9999932214850844, -0.33258196069982343)
COS_STEP = (1.999986449379199, -0.9969952843589359)


def horner(coefficients, x):
    total = coefficients[-1]
    for c in coefficients[-2::-1]:
        total = total * x + c
    return total


def split3(x):
    high = x.astype(BF16).astype(F32)
    rest = x - high
    middle = rest.astype(BF16).astype(F32)
    return high, middle, rest - middle


def spread_kernel(vis_ref, place_ref, *out_refs):
    k = lax.axis_index("stn")
    for s, out_ref in zip((1, 3, 0), out_refs):
        out_ref[...] = vis_ref[:, lax.rem(k + s, 4)].astype(F32)
    out_refs[3][...] = place_ref[...]


def front_kernel(
    vis_hbm, assign_hbm, cat_hbm, st_hbm, order_hbm, flag_hbm, cal_hbm, *refs
):
    send_ref, place_ref, far_hbm, vis, own, cat, st, order, flag, cal, sem, wide, out_sem = refs
    c = lax.axis_index("chan")
    k = lax.axis_index("stn")
    copies = [
        pltpu.make_async_copy(source, target, sem.at[i])
        for i, (source, target) in enumerate(
            (
                (st_hbm, st),
                (order_hbm, order),
                (flag_hbm, flag),
                (assign_hbm.at[pl.ds(pl.multiple_of(c * 8, 8), 8)], own),
                (cat_hbm, cat),
                (vis_hbm.at[:, lax.rem(k + 2, 4)], vis),
                (cal_hbm, cal),
            )
        )
    ]
    for copy in copies:
        copy.start()
    n = order.shape[1]
    for copy in copies[:3] + copies[6:]:
        copy.wait()
    hot = (lax.broadcasted_iota(jnp.int32, (n, n), 0) == order[...]).astype(F32).astype(BF16)
    high, middle, low = split3(st[...])
    rows = jnp.concatenate([high, middle, low, flag[...].astype(F32), jnp.zeros((9, n), F32)], axis=0)
    placed = jnp.dot(rows.astype(BF16), hot, preferred_element_type=F32)
    middle_nu = 1.0 + (4.0 * c.astype(F32) + 1.5) * (1.0 / 512.0)
    place_ref[...] = jnp.zeros_like(place_ref)
    place_ref[0:1] = placed[6:7]
    for ch in range(4):
        place_ref[4 + ch : 5 + ch] = jnp.broadcast_to(cal[:, ch : ch + 1], (1, n))
    place_ref[1:2] = (placed[0:1] + placed[2:3] + placed[4:5]) * middle_nu
    place_ref[2:3] = (placed[1:2] + placed[3:4] + placed[5:6]) * middle_nu
    copies[5].wait()
    wide[...] = vis[...].astype(F32)
    out = pltpu.make_async_copy(wide, far_hbm, out_sem)
    out.start()
    for copy in copies[3:5]:
        copy.wait()
    blocks = lax.broadcasted_iota(jnp.int32, (64, 128), 0)
    hits = [(blocks == own[t : t + 1]).astype(F32) for t in range(8)]
    stacked = jnp.concatenate(hits, axis=0).astype(BF16)
    upper = lax.broadcasted_iota(jnp.int32, (128, 128), 0) <= lax.broadcasted_iota(jnp.int32, (128, 128), 1)
    running = jnp.dot(stacked, upper.astype(F32).astype(BF16), preferred_element_type=F32)
    totals = jnp.dot(stacked, jnp.ones((128, 128), BF16), preferred_element_type=F32)
    before = jnp.full((64, 128), -1.0, F32)
    slot = lax.broadcasted_iota(jnp.int32, (CAP, 128), 0).astype(F32)
    pieces = split3(cat[...])
    left, right = [], []
    for t in range(8):
        part = slice(64 * t, 64 * t + 64)
        rank = jnp.sum(hits[t] * (running[part] + before), axis=0, keepdims=True)
        before = before + totals[part]
        chosen = slot == rank
        hit = hits[t].astype(BF16)
        for piece in pieces:
            left.append(hit)
            here = piece[:, 128 * t : 128 * t + 128]
            right.append(
                jnp.concatenate([jnp.where(chosen, here[f : f + 1], 0.0) for f in range(5)], axis=0).astype(BF16)
            )
    sent = lax.dot_general(
        jnp.concatenate(left, axis=1), jnp.concatenate(right, axis=1), NT, preferred_element_type=F32
    )
    send_ref[:, 0, :] = sent
    out.wait()


def phasor_kernel(
    recv_ref, place_ref, right_even, right_odd, left_out, model_ref, parts, spots, bright_rows, lefts, wides, sems
):
    rights = (right_even, right_odd)
    c = lax.axis_index("chan")
    k = lax.axis_index("stn")
    n = model_ref.shape[1]
    quarter = n // 4
    width = 256
    pairs = right_even.shape[0]
    tiles = width // 128
    base = 1.0 + 4.0 * c.astype(F32) * (1.0 / 512.0)
    middle_nu = 1.0 + (4.0 * c.astype(F32) + 1.5) * (1.0 / 512.0)
    step = jnp.full((8, width), 2.0 * jnp.pi / 1024.0, F32) / middle_nu
    sin1_by, sin3_by, cos2_by = SIN_STEP[0] * step, SIN_STEP[1] * step * step * step, COS_STEP[1] * step * step

    got = recv_ref[:, 0, :]
    got = jnp.concatenate([got, jnp.zeros((64, 256 - got.shape[1]), F32)], axis=1)
    got = jnp.concatenate([got, jnp.zeros((64, 256), F32)], axis=0).T
    lane = lax.broadcasted_iota(jnp.int32, (16, 128), 1)
    rows = []
    for f in range(5):
        low, high = got[32 * f : 32 * f + 16], got[32 * f + 16 : 32 * f + 32]
        rows.append(jnp.where(lane < 64, low, pltpu.roll(high, 64, 1)))
    parts[0] = rows[0]
    parts[1] = rows[1]
    for ch in range(4):
        log_nu = jnp.log(jnp.full((16, 128), 1.0, F32) * (base + ch / 512.0))
        parts[2 + ch] = rows[2] * jnp.exp(log_nu * (rows[3] + rows[4] * log_nu))

    for axis in range(2):
        for b in range(n // 128):
            row = place_ref[1 + axis : 2 + axis, 128 * b : 128 * b + 128]
            spots[axis, 128 * b : 128 * b + 128] = jnp.broadcast_to(row, (128, 128)).T

    def out_copy(chunk, buffer):
        return pltpu.make_async_copy(
            lefts[buffer].at[:, pl.ds(pl.multiple_of(k * quarter, quarter), quarter)],
            left_out.at[chunk],
            sems.at[buffer],
        )

    def phases(buffer, r0, g):
        right, left, wide = rights[buffer].at[g], lefts[buffer], wides[buffer]
        rows = slice(r0, r0 + 8)
        x = jnp.concatenate([spots[0, rows]] * tiles, axis=1)
        y = jnp.concatenate([spots[1, rows]] * tiles, axis=1)
        turns = wide[0] * x + wide[1] * y
        r = turns - jnp.round(turns)
        t = r * r
        s = r * horner(SIN_HALF, t)
        h = horner(COS_HALF, t)
        half_cos = 0.5 - s * s
        half_sin = s * h
        square = turns * turns
        s2 = turns * (sin1_by + sin3_by * square)
        c2 = COS_STEP[0] + cos2_by * square
        twice = 2.0 - s2 * s2
        cc, ss = half_cos * c2, half_sin * s2
        sc, cs = half_sin * c2, half_cos * s2
        cos1, cos2 = cc + ss, cc - ss
        sin1, sin2 = sc - cs, sc + cs
        for ch, cosine, sine in (
            (1, cos1, sin1),
            (2, cos2, sin2),
            (0, twice * cos1 - cos2, twice * sin1 - sin2),
            (3, twice * cos2 - cos1, twice * sin2 - sin1),
        ):
            bright = wide[2 + ch]
            right[ch, rows, :width] = (bright * cosine).astype(BF16)
            right[ch, rows, width:] = (bright * sine).astype(BF16)
            left[ch, rows, :width] = cosine.astype(BF16)
            left[ch, rows, width:] = sine.astype(BF16)

    lefts[1][k] = jnp.zeros((n, 2 * width), BF16)
    right_odd[pairs - 1, k] = jnp.zeros((n, 2 * width), BF16)

    def chunks(*totals):
        def matmul(other, turn, block, g):
            left, right = lefts[other], rights[other].at[g]
            columns = slice(turn * width, turn * width + width)
            if block == 0:
                for half in range(2):
                    pltpu.matmul_push_rhs(
                        right[k, half * width : half * width + width, columns], turn, half, transpose=True
                    )
            rows = slice(128 * (block % 4), 128 * (block % 4) + 128)
            if block < 4:
                lhs = left[k, rows, columns]
            else:
                lhs = left[k, rows, (1 - turn) * width : (2 - turn) * width]
                if turn == 1:
                    lhs = -lhs
            for half in range(2):
                pltpu.matmul_acc_lhs(totals[8 * half + block], lhs, turn if block == 0 else None)

        def pair(g, _):
            for sub in range(2):
                chunk = 2 * g + sub

                @pl.when(g > 0)
                def _():
                    out_copy(chunk - 2, sub).wait()

                for f in range(6):
                    for j in range(tiles):
                        row = parts[f, pl.ds(tiles * chunk + j, 1)]
                        wides[sub][f, :, 128 * j : 128 * j + 128] = jnp.broadcast_to(row, (8, 128))
                for turn in range(2):
                    for block in range(8):

                        def body(sub=sub, turn=turn, block=block):
                            matmul(1 - sub, turn, block, g if sub else lax.rem(g + pairs - 1, pairs))
                            for i in range(4):
                                phases(sub, 32 * (8 * turn + block) + 8 * i, g)

                        pl.when(g >= 0)(body)
                out_copy(chunk, sub).start()
            return 0

        lax.fori_loop(0, pairs, pair, 0)
        for turn in range(2):
            for block in range(8):
                matmul(1, turn, block, pairs - 1)
        for sub in range(2):
            out_copy(2 * pairs - 2 + sub, sub).wait()
        bright_rows[0:4] = place_ref[4:8, :128]
        bright = bright_rows[pl.ds(k, 1)]
        bright = jnp.concatenate([bright, bright], axis=1)
        off = lax.broadcasted_iota(jnp.int32, (128, 128), 0) != lax.broadcasted_iota(jnp.int32, (128, 128), 1)
        for block in range(8):
            rows = slice(128 * block, 128 * block + 128)
            for half in range(2):
                total = pltpu.matmul_pop(totals[8 * half + block])
                if block < 4:
                    total = total + bright
                for j in range(2):
                    part = total[:, 128 * j : 128 * j + 128]
                    column = 2 * half + j
                    if column == block % 4:
                        part = jnp.where(off, part, 0.0)
                    model_ref[rows, 128 * column : 128 * column + 128] = part

    pl.run_scoped(chunks, *[pltpu.ACC(half)((128, 256), F32) for half in range(2) for _ in range(8)])


def model_kernel(right_even, right_odd, left_ref, own_ref, place_ref, model_ref, wide):
    k = lax.axis_index("stn")
    chunks, rows, half = left_ref.shape[0], left_ref.shape[2], left_ref.shape[3] // 2
    wide[0:4] = place_ref[4:8, :128]
    first = pl.multiple_of(k * rows, rows)
    model_ref[k, :rows] = own_ref[pl.ds(first, rows)]
    model_ref[k, rows:] = own_ref[pl.ds(4 * rows + first, rows)]

    def channel(i, _):
        ch = lax.rem(k + 1 + i, 4)
        lefts = []
        for q in range(chunks):
            left = left_ref[q, ch]
            cosine, sine = left[:, :half], left[:, half:]
            lefts.append(jnp.concatenate([left, jnp.concatenate([sine, -cosine], axis=1)], axis=0))
        total = lax.dot_general(
            jnp.concatenate(lefts, axis=1),
            jnp.concatenate([(right_even, right_odd)[q % 2][q // 2, ch] for q in range(chunks)], axis=1),
            NT,
            preferred_element_type=F32,
        )
        bright = jnp.concatenate([wide[pl.ds(ch, 1)]] * 4, axis=1)
        model_ref[ch, :rows] = total[:rows] + bright
        model_ref[ch, rows:] = total[rows:]
        return 0

    lax.fori_loop(0, 3, channel, 0)


def solve_kernel(model_ref, v0, v1, v2, v3, ok_ref, out_ref, a_re, a_im, b_ab, wide, part):
    k = lax.axis_index("stn")
    n = v0.shape[2]
    quarter = n // 4
    ok = ok_ref[0:1]

    def fold(x):
        return (x[:, :128] + x[:, 128:256]) + (x[:, 256:384] + x[:, 384:])

    def set_up(s, v):
        first = lax.rem(k + 4 - s, 4) * quarter

        def body(i, _):
            local = pl.multiple_of(8 * i, 8)
            r0 = pl.multiple_of(first + 8 * i, 8)
            mr = model_ref[pl.ds(r0, 8)]
            mi = model_ref[pl.ds(n + r0, 8)]
            vr = v[0, pl.ds(local, 8)]
            vi = v[1, pl.ds(local, 8)]
            ar = mr * vr + mi * vi
            ai = mr * vi - mi * vr
            b = mr * mr + mi * mi
            a_re[pl.ds(r0, 8)] = ar
            a_im[pl.ds(r0, 8)] = ai
            b_ab[pl.ds(r0, 8)] = b
            g = wide[0]
            part[0, pl.ds(r0, 8)] = fold(ar * g)
            part[1, pl.ds(r0, 8)] = fold(ai * g)
            part[2, pl.ds(r0, 8)] = fold(b * g)
            return 0

        lax.fori_loop(0, quarter // 8, body, 0, unroll=4)

    def sums():
        gr, gi, gg = wide[0], wide[1], wide[2]

        def body(i, _):
            r0 = pl.multiple_of(8 * i, 8)
            ar, ai = a_re[pl.ds(r0, 8)], a_im[pl.ds(r0, 8)]
            part[0, pl.ds(r0, 8)] = fold(ar * gr - ai * gi)
            part[1, pl.ds(r0, 8)] = fold(ar * gi + ai * gr)
            part[2, pl.ds(r0, 8)] = fold(b_ab[pl.ds(r0, 8)] * gg)
            return 0

        lax.fori_loop(0, n // 8, body, 0, unroll=4)

    def total(q):
        return jnp.concatenate(
            [jnp.sum(part[q, 128 * b : 128 * b + 128].T, axis=0, keepdims=True) for b in range(n // 128)], axis=1
        )

    g_re, g_im = jnp.ones((1, n), F32), jnp.zeros((1, n), F32)
    out_ref[...] = jnp.zeros_like(out_ref)
    for iteration in range(ITERS):
        wide[0] = jnp.broadcast_to(ok * g_re, (8, n))
        wide[1] = jnp.broadcast_to(ok * g_im, (8, n))
        wide[2] = jnp.broadcast_to(ok * (g_re * g_re + g_im * g_im), (8, n))
        if iteration == 0:
            for s, v in enumerate((v0, v1, v2, v3)):
                set_up(s, v)
        else:
            sums()
        below = total(2) * ok + 1e-6 + (1.0 - ok)
        new_re = total(0) * ok / below
        new_im = total(1) * ok / below
        if iteration % 2 == 1:
            new_re = 0.5 * (new_re + g_re)
            new_im = 0.5 * (new_im + g_im)
        moved = jnp.sum((new_re - g_re) ** 2 + (new_im - g_im) ** 2, axis=1, keepdims=True)
        size = jnp.sum(new_re * new_re + new_im * new_im, axis=1, keepdims=True)
        out_ref[2 + iteration : 3 + iteration] = jnp.broadcast_to(moved / (size + 1e-6), (1, n))
        g_re, g_im = new_re, new_im
    out_ref[0:1] = g_re
    out_ref[1:2] = g_im


def residual_kernel(model_ref, vis_ref, g0, g1, g2, g3, ok_ref, gains_ref, res_ref, change_ref, table):
    k = lax.axis_index("stn")
    ch = pl.program_id(0)
    n = vis_ref.shape[3]
    quarter = n // 4
    lanes = pl.ds(pl.multiple_of(k * quarter, 128), quarter)

    @pl.when(ch == 0)
    def _():
        for s, g in enumerate((g0, g1, g2, g3)):
            table[lax.rem(k + 4 - s, 4)] = g[...]
        lane = lax.broadcasted_iota(jnp.int32, (ITERS, 4), 1)
        history = jnp.zeros((ITERS, 4), F32)
        for q in range(4):
            gains_ref[0, q : q + 1] = table[q, 0:1, lanes]
            gains_ref[1, q : q + 1] = table[q, 1:2, lanes]
            history = jnp.where(lane == q, table[q, 2 : 2 + ITERS, 0:4], history)
        change_ref[...] = history

    def column(row):
        return jnp.broadcast_to(row, (128, 128)).T

    gi_re = column(table[ch, 0:1, lanes])
    gi_im = column(table[ch, 1:2, lanes])
    ui = column(ok_ref[0:1, lanes])
    columns = lax.broadcasted_iota(jnp.int32, (16, 128), 1)
    sub = lax.broadcasted_iota(jnp.int32, (16, 128), 0)
    gj_re = [jnp.broadcast_to(table[ch, 0:1, 128 * b : 128 * b + 128], (16, 128)) for b in range(4)]
    gj_im = [jnp.broadcast_to(table[ch, 1:2, 128 * b : 128 * b + 128], (16, 128)) for b in range(4)]
    uj = [jnp.broadcast_to(ok_ref[0:1, 128 * b : 128 * b + 128], (16, 128)) for b in range(4)]
    for i in range(quarter // 16):
        rows = slice(16 * i, 16 * i + 16)
        a_re, a_im, a_ok = gi_re[rows], gi_im[rows], ui[rows]
        for b in range(4):
            at = slice(128 * b, 128 * b + 128)
            off = columns + 128 * b != sub + (k * quarter + 16 * i)
            e = jnp.where(off, a_ok * uj[b], 0.0)
            p_re = a_re * gj_re[b] + a_im * gj_im[b]
            p_im = a_im * gj_re[b] - a_re * gj_im[b]
            mr = model_ref[ch, rows, at]
            mi = model_ref[ch, slice(quarter + 16 * i, quarter + 16 * i + 16), at]
            vr = vis_ref[0, ch, rows, at].astype(F32)
            vi = vis_ref[1, ch, rows, at].astype(F32)
            res_ref[0, 0, rows, at] = (e * (vr - (p_re * mr - p_im * mi))).astype(BF16)
            res_ref[1, 0, rows, at] = (e * (vi - (p_re * mi + p_im * mr))).astype(BF16)


def per_device(visibilities, calibrator, catalog, assignment, stations, input_order, station_flags):
    rows, n = visibilities.shape[2], visibilities.shape[3]
    sources = 64 * CAP
    chunks = sources // 256
    whole = pl.BlockSpec(memory_space=VMEM)
    hbm = pl.BlockSpec(memory_space=pltpu.HBM)
    small = pltpu.CompilerParams(vmem_limit_bytes=6 << 20)

    def shape(*dims, dtype=F32):
        return jax.ShapeDtypeStruct(dims, dtype)

    def ring(s):
        return [(i, (i + s) % 4) for i in range(4)]

    send, place, far = pl.pallas_call(
        front_kernel,
        out_shape=[shape(64, 1, 5 * CAP), shape(8, n), shape(2, rows, n)],
        in_specs=[hbm] * 7,
        out_specs=[whole] * 2 + [hbm],
        scratch_shapes=[
            VMEM((2, rows, n), BF16),
            VMEM((8, 128), jnp.int32),
            VMEM(catalog.shape, F32),
            VMEM(stations.shape, F32),
            VMEM((1, n), jnp.int32),
            VMEM((1, n), jnp.int32),
            VMEM((1, 4), F32),
            pltpu.SemaphoreType.DMA((7,)),
            VMEM((2, rows, n), F32),
            pltpu.SemaphoreType.DMA,
        ],
        name="front",
    )(
        visibilities,
        assignment.reshape(-1, 128),
        catalog,
        stations,
        input_order.reshape(1, n),
        station_flags.reshape(1, n),
        calibrator.reshape(1, 4),
    )

    ahead, behind, own, place = pl.pallas_call(
        spread_kernel,
        out_shape=[shape(2, rows, n)] * 3 + [shape(8, n)],
        in_specs=[whole] * 2,
        out_specs=[whole] * 4,
        compiler_params=small,
        cost_estimate=pl.CostEstimate(flops=1 << 20, bytes_accessed=2 << 20, transcendentals=0),
        name="spread",
    )(visibilities, place)

    def turn(tile, s):
        return lax.ppermute(tile, "stn", ring(s))

    received = lax.all_to_all(send, "chan", 0, 0)
    tiles = [own, turn(ahead, 1), turn(far, 2), turn(behind, 3)]

    right_even, right_odd, left, model_own = pl.pallas_call(
        phasor_kernel,
        out_shape=[
            shape(chunks // 2, 4, n, 512, dtype=BF16),
            shape(chunks // 2, 4, n, 512, dtype=BF16),
            shape(chunks, 4, rows, 512, dtype=BF16),
            shape(2 * n, n),
        ],
        in_specs=[whole] * 2,
        out_specs=[whole, whole, hbm, whole],
        scratch_shapes=[
            VMEM((6, 16, 128), F32),
            VMEM((2, n, 128), F32),
            VMEM((8, 128), F32),
            [VMEM((4, n, 512), BF16)] * 2,
            [VMEM((6, 8, 256), F32)] * 2,
            pltpu.SemaphoreType.DMA((2,)),
        ],
        compiler_params=pltpu.CompilerParams(vmem_limit_bytes=8 << 20),
        cost_estimate=pl.CostEstimate(flops=10 << 30, bytes_accessed=21 << 20, transcendentals=0),
        name="phasor",
    )(received, place)

    solved = pl.pallas_call(
        solve_kernel,
        out_shape=shape(8, n),
        in_specs=[whole] * 6,
        out_specs=whole,
        scratch_shapes=[VMEM((n, n), F32)] * 3 + [VMEM((3, 8, n), F32), VMEM((3, n, 128), F32)],
        compiler_params=small,
        name="solve",
    )(model_own, *tiles, place)
    tables = [solved] + [lax.ppermute(solved, "stn", ring(s)) for s in (1, 2, 3)]

    model = pl.pallas_call(
        model_kernel,
        out_shape=shape(4, 2 * rows, n),
        in_specs=[whole] * 5,
        out_specs=whole,
        scratch_shapes=[VMEM((8, 128), F32)],
        compiler_params=small,
        cost_estimate=pl.CostEstimate(flops=4 << 30, bytes_accessed=21 << 20, transcendentals=0),
        name="model",
    )(right_even, right_odd, left, model_own, place)

    gains, residual, changes = pl.pallas_call(
        residual_kernel,
        grid=(4,),
        out_shape=[shape(2, 4, rows), shape(2, 4, rows, n, dtype=BF16), shape(ITERS, 4)],
        in_specs=[whole] * 7,
        out_specs=[
            pl.BlockSpec((2, 4, rows), lambda q: (0, 0, 0)),
            pl.BlockSpec((2, 1, rows, n), lambda q: (0, q, 0, 0)),
            pl.BlockSpec((ITERS, 4), lambda q: (0, 0)),
        ],
        scratch_shapes=[VMEM((4, 8, n), F32)],
        compiler_params=small,
        name="residual",
    )(model, visibilities, *tables, place)
    return (gains, residual, changes)


def solution(mesh):
    placed = (P(None, "chan", "stn", None), P("chan"), P(None, "chan"), P(), P(), P(), P())

    return jax.shard_map(
        per_device,
        mesh=mesh,
        in_specs=placed,
        out_specs=(P(None, "chan", "stn"), P(None, "chan", "stn", None), P(None, "chan")),
        check_vma=False,
    )
```

```python
import jax
import jax.numpy as jnp
from jax import lax
from jax.experimental import pallas as pl
from jax.experimental.pallas import tpu as pltpu
from jax.sharding import PartitionSpec as P


ITERS = 3
CAP = 32
VMEM = pltpu.VMEM
F32 = jnp.float32
BF16 = jnp.bfloat16
NT = (((1,), (1,)), ((), ()))

SIN_HALF = (3.141582005383235, -5.167142124470761, 2.541892570102862, -0.5546189642693115)
COS_HALF = (0.9999932847330446, -4.93393699910271, 4.041270253370243, -1.2220835776975139)
SIN_STEP = (1.9999932214850844, -0.33258196069982343)
COS_STEP = (1.999986449379199, -0.9969952843589359)


def horner(coefficients, x):
    total = coefficients[-1]
    for c in coefficients[-2::-1]:
        total = total * x + c
    return total


def split3(x):
    high = x.astype(BF16).astype(F32)
    rest = x - high
    middle = rest.astype(BF16).astype(F32)
    return high, middle, rest - middle


def spread_kernel(vis_ref, place_ref, *out_refs):
    k = lax.axis_index("stn")
    for s, out_ref in zip((2, 0), out_refs):
        out_ref[...] = vis_ref[:, lax.rem(k + s, 4)].astype(F32)
    out_refs[2][...] = place_ref[...]


def front_kernel(
    vis_hbm, assign_hbm, cat_hbm, st_hbm, order_hbm, flag_hbm, cal_hbm, *refs
):
    send_hbm, place_ref, ahead_hbm, behind_hbm, vis, own, cat, st, order, flag, cal, sem, wide, send, out_sem = refs
    c = lax.axis_index("chan")
    k = lax.axis_index("stn")
    copies = [
        pltpu.make_async_copy(source, target, sem.at[i])
        for i, (source, target) in enumerate(
            (
                (st_hbm, st),
                (order_hbm, order),
                (flag_hbm, flag),
                (assign_hbm.at[pl.ds(pl.multiple_of(c * 8, 8), 8)], own),
                (cat_hbm, cat),
                (vis_hbm.at[:, lax.rem(k + 1, 4)], vis.at[0]),
                (cal_hbm, cal),
                (vis_hbm.at[:, lax.rem(k + 3, 4)], vis.at[1]),
            )
        )
    ]
    for i in (5, 7, 3, 4, 0, 1, 2, 6):
        copies[i].start()
    n = order.shape[1]
    outs = []
    for i, tile_hbm in enumerate((ahead_hbm, behind_hbm)):
        copies[5 + 2 * i].wait()
        wide[i] = vis[i].astype(F32)
        outs.append(pltpu.make_async_copy(wide.at[i], tile_hbm, out_sem.at[i]))
        outs[-1].start()
    for copy in copies[3:5]:
        copy.wait()
    blocks = lax.broadcasted_iota(jnp.int32, (64, 128), 0)
    hits = [(blocks == own[t : t + 1]).astype(F32) for t in range(8)]
    stacked = jnp.concatenate(hits, axis=0).astype(BF16)
    upper = lax.broadcasted_iota(jnp.int32, (128, 128), 0) <= lax.broadcasted_iota(jnp.int32, (128, 128), 1)
    running = jnp.dot(stacked, upper.astype(F32).astype(BF16), preferred_element_type=F32)
    totals = jnp.dot(stacked, jnp.ones((128, 128), BF16), preferred_element_type=F32)
    before = jnp.full((64, 128), -1.0, F32)
    slot = lax.broadcasted_iota(jnp.int32, (CAP, 128), 0).astype(F32)
    pieces = split3(cat[...])
    left, right = [], []
    for t in range(8):
        part = slice(64 * t, 64 * t + 64)
        rank = jnp.sum(hits[t] * (running[part] + before), axis=0, keepdims=True)
        before = before + totals[part]
        chosen = slot == rank
        hit = hits[t].astype(BF16)
        for piece in pieces:
            left.append(hit)
            here = piece[:, 128 * t : 128 * t + 128]
            right.append(
                jnp.concatenate([jnp.where(chosen, here[f : f + 1], 0.0) for f in range(5)], axis=0).astype(BF16)
            )
    sent = lax.dot_general(
        jnp.concatenate(left, axis=1), jnp.concatenate(right, axis=1), NT, preferred_element_type=F32
    )
    send[:, 0, :] = sent
    sending = pltpu.make_async_copy(send, send_hbm, out_sem.at[2])
    sending.start()
    for copy in copies[:3] + copies[6:7]:
        copy.wait()
    hot = (lax.broadcasted_iota(jnp.int32, (n, n), 0) == order[...]).astype(F32).astype(BF16)
    high, middle, low = split3(st[...])
    rows = jnp.concatenate([high, middle, low, flag[...].astype(F32), jnp.zeros((9, n), F32)], axis=0)
    placed = jnp.dot(rows.astype(BF16), hot, preferred_element_type=F32)
    middle_nu = 1.0 + (4.0 * c.astype(F32) + 1.5) * (1.0 / 512.0)
    place_ref[...] = jnp.zeros_like(place_ref)
    place_ref[0:1] = placed[6:7]
    for ch in range(4):
        place_ref[4 + ch : 5 + ch] = jnp.broadcast_to(cal[:, ch : ch + 1], (1, n))
    place_ref[1:2] = (placed[0:1] + placed[2:3] + placed[4:5]) * middle_nu
    place_ref[2:3] = (placed[1:2] + placed[3:4] + placed[5:6]) * middle_nu
    for out in outs:
        out.wait()
    sending.wait()


def phasor_kernel(
    recv_ref, place_ref, right_even, right_odd, left_out, model_ref, parts, spots, bright_rows, lefts, wides, sems
):
    rights = (right_even, right_odd)
    c = lax.axis_index("chan")
    k = lax.axis_index("stn")
    n = model_ref.shape[1]
    quarter = n // 4
    width = 256
    pairs = right_even.shape[0]
    tiles = width // 128
    base = 1.0 + 4.0 * c.astype(F32) * (1.0 / 512.0)
    middle_nu = 1.0 + (4.0 * c.astype(F32) + 1.5) * (1.0 / 512.0)
    step = jnp.full((8, width), 2.0 * jnp.pi / 1024.0, F32) / middle_nu
    sin1_by, sin3_by, cos2_by = SIN_STEP[0] * step, SIN_STEP[1] * step * step * step, COS_STEP[1] * step * step

    got = recv_ref[:, 0, :]
    got = jnp.concatenate([got, jnp.zeros((64, 256 - got.shape[1]), F32)], axis=1)
    got = jnp.concatenate([got, jnp.zeros((64, 256), F32)], axis=0).T
    lane = lax.broadcasted_iota(jnp.int32, (16, 128), 1)
    rows = []
    for f in range(5):
        low, high = got[32 * f : 32 * f + 16], got[32 * f + 16 : 32 * f + 32]
        rows.append(jnp.where(lane < 64, low, pltpu.roll(high, 64, 1)))
    parts[0] = rows[0]
    parts[1] = rows[1]
    for ch in range(4):
        log_nu = jnp.log(jnp.full((16, 128), 1.0, F32) * (base + ch / 512.0))
        parts[2 + ch] = rows[2] * jnp.exp(log_nu * (rows[3] + rows[4] * log_nu))

    for axis in range(2):
        for b in range(n // 128):
            row = place_ref[1 + axis : 2 + axis, 128 * b : 128 * b + 128]
            spots[axis, 128 * b : 128 * b + 128] = jnp.broadcast_to(row, (128, 128)).T

    def out_copy(chunk, buffer):
        return pltpu.make_async_copy(
            lefts[buffer].at[:, pl.ds(pl.multiple_of(k * quarter, quarter), quarter)],
            left_out.at[chunk],
            sems.at[buffer],
        )

    def phases(buffer, r0, g):
        right, left, wide = rights[buffer].at[g], lefts[buffer], wides[buffer]
        rows = slice(r0, r0 + 8)
        x = jnp.concatenate([spots[0, rows]] * tiles, axis=1)
        y = jnp.concatenate([spots[1, rows]] * tiles, axis=1)
        turns = wide[0] * x + wide[1] * y
        r = turns - jnp.round(turns)
        t = r * r
        s = r * horner(SIN_HALF, t)
        h = horner(COS_HALF, t)
        half_cos = 0.5 - s * s
        half_sin = s * h
        square = turns * turns
        s2 = turns * (sin1_by + sin3_by * square)
        c2 = COS_STEP[0] + cos2_by * square
        twice = 2.0 - s2 * s2
        cc, ss = half_cos * c2, half_sin * s2
        sc, cs = half_sin * c2, half_cos * s2
        cos1, cos2 = cc + ss, cc - ss
        sin1, sin2 = sc - cs, sc + cs
        for ch, cosine, sine in (
            (1, cos1, sin1),
            (2, cos2, sin2),
            (0, twice * cos1 - cos2, twice * sin1 - sin2),
            (3, twice * cos2 - cos1, twice * sin2 - sin1),
        ):
            bright = wide[2 + ch]
            right[ch, rows, :width] = (bright * cosine).astype(BF16)
            right[ch, rows, width:] = (bright * sine).astype(BF16)
            left[ch, rows, :width] = cosine.astype(BF16)
            left[ch, rows, width:] = sine.astype(BF16)

    lefts[1][k] = jnp.zeros((n, 2 * width), BF16)
    right_odd[pairs - 1, k] = jnp.zeros((n, 2 * width), BF16)

    def chunks(*totals):
        def matmul(other, turn, block, g):
            left, right = lefts[other], rights[other].at[g]
            columns = slice(turn * width, turn * width + width)
            if block == 0:
                for half in range(2):
                    pltpu.matmul_push_rhs(
                        right[k, half * width : half * width + width, columns], turn, half, transpose=True
                    )
            rows = slice(128 * (block % 4), 128 * (block % 4) + 128)
            if block < 4:
                lhs = left[k, rows, columns]
            else:
                lhs = left[k, rows, (1 - turn) * width : (2 - turn) * width]
                if turn == 1:
                    lhs = -lhs
            for half in range(2):
                pltpu.matmul_acc_lhs(totals[8 * half + block], lhs, turn if block == 0 else None)

        def pair(g, _):
            for sub in range(2):
                chunk = 2 * g + sub

                @pl.when(g > 0)
                def _():
                    out_copy(chunk - 2, sub).wait()

                for f in range(6):
                    for j in range(tiles):
                        row = parts[f, pl.ds(tiles * chunk + j, 1)]
                        wides[sub][f, :, 128 * j : 128 * j + 128] = jnp.broadcast_to(row, (8, 128))
                for turn in range(2):
                    for block in range(8):

                        def body(sub=sub, turn=turn, block=block):
                            matmul(1 - sub, turn, block, g if sub else lax.rem(g + pairs - 1, pairs))
                            for i in range(4):
                                phases(sub, 32 * (8 * turn + block) + 8 * i, g)

                        pl.when(g >= 0)(body)
                out_copy(chunk, sub).start()
            return 0

        lax.fori_loop(0, pairs, pair, 0)
        for turn in range(2):
            for block in range(8):
                matmul(1, turn, block, pairs - 1)
        for sub in range(2):
            out_copy(2 * pairs - 2 + sub, sub).wait()
        bright_rows[0:4] = place_ref[4:8, :128]
        bright = bright_rows[pl.ds(k, 1)]
        bright = jnp.concatenate([bright, bright], axis=1)
        off = lax.broadcasted_iota(jnp.int32, (128, 128), 0) != lax.broadcasted_iota(jnp.int32, (128, 128), 1)
        for block in range(8):
            rows = slice(128 * block, 128 * block + 128)
            for half in range(2):
                total = pltpu.matmul_pop(totals[8 * half + block])
                if block < 4:
                    total = total + bright
                for j in range(2):
                    part = total[:, 128 * j : 128 * j + 128]
                    column = 2 * half + j
                    if column == block % 4:
                        part = jnp.where(off, part, 0.0)
                    model_ref[rows, 128 * column : 128 * column + 128] = part

    pl.run_scoped(chunks, *[pltpu.ACC(half)((128, 256), F32) for half in range(2) for _ in range(8)])


def model_kernel(right_even, right_odd, left_ref, own_ref, place_ref, model_ref, wide):
    k = lax.axis_index("stn")
    chunks, rows, half = left_ref.shape[0], left_ref.shape[2], left_ref.shape[3] // 2
    wide[0:4] = place_ref[4:8, :128]
    first = pl.multiple_of(k * rows, rows)
    model_ref[k, :rows] = own_ref[pl.ds(first, rows)]
    model_ref[k, rows:] = own_ref[pl.ds(4 * rows + first, rows)]

    def channel(i, _):
        ch = lax.rem(k + 1 + i, 4)
        lefts = []
        for q in range(chunks):
            left = left_ref[q, ch]
            cosine, sine = left[:, :half], left[:, half:]
            lefts.append(jnp.concatenate([left, jnp.concatenate([sine, -cosine], axis=1)], axis=0))
        total = lax.dot_general(
            jnp.concatenate(lefts, axis=1),
            jnp.concatenate([(right_even, right_odd)[q % 2][q // 2, ch] for q in range(chunks)], axis=1),
            NT,
            preferred_element_type=F32,
        )
        bright = jnp.concatenate([wide[pl.ds(ch, 1)]] * 4, axis=1)
        model_ref[ch, :rows] = total[:rows] + bright
        model_ref[ch, rows:] = total[rows:]
        return 0

    lax.fori_loop(0, 3, channel, 0)


def solve_kernel(model_ref, v0, v1, v2, v3, ok_ref, out_ref, a_re, a_im, b_ab, wide, part):
    k = lax.axis_index("stn")
    n = v0.shape[2]
    quarter = n // 4
    ok = ok_ref[0:1]

    def fold(x):
        return (x[:, :128] + x[:, 128:256]) + (x[:, 256:384] + x[:, 384:])

    def set_up(s, v):
        first = lax.rem(k + 4 - s, 4) * quarter

        def body(i, _):
            local = pl.multiple_of(8 * i, 8)
            r0 = pl.multiple_of(first + 8 * i, 8)
            mr = model_ref[pl.ds(r0, 8)]
            mi = model_ref[pl.ds(n + r0, 8)]
            vr = v[0, pl.ds(local, 8)]
            vi = v[1, pl.ds(local, 8)]
            ar = mr * vr + mi * vi
            ai = mr * vi - mi * vr
            b = mr * mr + mi * mi
            a_re[pl.ds(r0, 8)] = ar
            a_im[pl.ds(r0, 8)] = ai
            b_ab[pl.ds(r0, 8)] = b
            g = wide[0]
            part[0, pl.ds(r0, 8)] = fold(ar * g)
            part[1, pl.ds(r0, 8)] = fold(ai * g)
            part[2, pl.ds(r0, 8)] = fold(b * g)
            return 0

        lax.fori_loop(0, quarter // 8, body, 0, unroll=4)

    def sums():
        gr, gi, gg = wide[0], wide[1], wide[2]

        def body(i, _):
            r0 = pl.multiple_of(8 * i, 8)
            ar, ai = a_re[pl.ds(r0, 8)], a_im[pl.ds(r0, 8)]
            part[0, pl.ds(r0, 8)] = fold(ar * gr - ai * gi)
            part[1, pl.ds(r0, 8)] = fold(ar * gi + ai * gr)
            part[2, pl.ds(r0, 8)] = fold(b_ab[pl.ds(r0, 8)] * gg)
            return 0

        lax.fori_loop(0, n // 8, body, 0, unroll=4)

    def total(q):
        return jnp.concatenate(
            [jnp.sum(part[q, 128 * b : 128 * b + 128].T, axis=0, keepdims=True) for b in range(n // 128)], axis=1
        )

    g_re, g_im = jnp.ones((1, n), F32), jnp.zeros((1, n), F32)
    out_ref[...] = jnp.zeros_like(out_ref)
    for iteration in range(ITERS):
        wide[0] = jnp.broadcast_to(ok * g_re, (8, n))
        wide[1] = jnp.broadcast_to(ok * g_im, (8, n))
        wide[2] = jnp.broadcast_to(ok * (g_re * g_re + g_im * g_im), (8, n))
        if iteration == 0:
            for s, v in enumerate((v0, v1, v2, v3)):
                set_up(s, v)
        else:
            sums()
        below = total(2) * ok + 1e-6 + (1.0 - ok)
        new_re = total(0) * ok / below
        new_im = total(1) * ok / below
        if iteration % 2 == 1:
            new_re = 0.5 * (new_re + g_re)
            new_im = 0.5 * (new_im + g_im)
        moved = jnp.sum((new_re - g_re) ** 2 + (new_im - g_im) ** 2, axis=1, keepdims=True)
        size = jnp.sum(new_re * new_re + new_im * new_im, axis=1, keepdims=True)
        out_ref[2 + iteration : 3 + iteration] = jnp.broadcast_to(moved / (size + 1e-6), (1, n))
        g_re, g_im = new_re, new_im
    out_ref[0:1] = g_re
    out_ref[1:2] = g_im


def residual_kernel(model_ref, vis_ref, g0, g1, g2, g3, ok_ref, gains_ref, res_ref, change_ref, table):
    k = lax.axis_index("stn")
    ch = pl.program_id(0)
    n = vis_ref.shape[3]
    quarter = n // 4
    lanes = pl.ds(pl.multiple_of(k * quarter, 128), quarter)

    @pl.when(ch == 0)
    def _():
        for s, g in enumerate((g0, g1, g2, g3)):
            table[lax.rem(k + 4 - s, 4)] = g[...]
        lane = lax.broadcasted_iota(jnp.int32, (ITERS, 4), 1)
        history = jnp.zeros((ITERS, 4), F32)
        for q in range(4):
            gains_ref[0, q : q + 1] = table[q, 0:1, lanes]
            gains_ref[1, q : q + 1] = table[q, 1:2, lanes]
            history = jnp.where(lane == q, table[q, 2 : 2 + ITERS, 0:4], history)
        change_ref[...] = history

    def column(row):
        return jnp.broadcast_to(row, (128, 128)).T

    gi_re = column(table[ch, 0:1, lanes])
    gi_im = column(table[ch, 1:2, lanes])
    ui = column(ok_ref[0:1, lanes])
    columns = lax.broadcasted_iota(jnp.int32, (16, 128), 1)
    sub = lax.broadcasted_iota(jnp.int32, (16, 128), 0)
    gj_re = [jnp.broadcast_to(table[ch, 0:1, 128 * b : 128 * b + 128], (16, 128)) for b in range(4)]
    gj_im = [jnp.broadcast_to(table[ch, 1:2, 128 * b : 128 * b + 128], (16, 128)) for b in range(4)]
    uj = [jnp.broadcast_to(ok_ref[0:1, 128 * b : 128 * b + 128], (16, 128)) for b in range(4)]
    for i in range(quarter // 16):
        rows = slice(16 * i, 16 * i + 16)
        a_re, a_im, a_ok = gi_re[rows], gi_im[rows], ui[rows]
        for b in range(4):
            at = slice(128 * b, 128 * b + 128)
            off = columns + 128 * b != sub + (k * quarter + 16 * i)
            e = jnp.where(off, a_ok * uj[b], 0.0)
            p_re = a_re * gj_re[b] + a_im * gj_im[b]
            p_im = a_im * gj_re[b] - a_re * gj_im[b]
            mr = model_ref[ch, rows, at]
            mi = model_ref[ch, slice(quarter + 16 * i, quarter + 16 * i + 16), at]
            vr = vis_ref[0, ch, rows, at].astype(F32)
            vi = vis_ref[1, ch, rows, at].astype(F32)
            res_ref[0, 0, rows, at] = (e * (vr - (p_re * mr - p_im * mi))).astype(BF16)
            res_ref[1, 0, rows, at] = (e * (vi - (p_re * mi + p_im * mr))).astype(BF16)


def per_device(visibilities, calibrator, catalog, assignment, stations, input_order, station_flags):
    rows, n = visibilities.shape[2], visibilities.shape[3]
    sources = 64 * CAP
    chunks = sources // 256
    whole = pl.BlockSpec(memory_space=VMEM)
    hbm = pl.BlockSpec(memory_space=pltpu.HBM)
    small = pltpu.CompilerParams(vmem_limit_bytes=6 << 20)

    def shape(*dims, dtype=F32):
        return jax.ShapeDtypeStruct(dims, dtype)

    def ring(s):
        return [(i, (i + s) % 4) for i in range(4)]

    send, place, ahead, behind = pl.pallas_call(
        front_kernel,
        out_shape=[shape(64, 1, 5 * CAP), shape(8, n)] + [shape(2, rows, n)] * 2,
        in_specs=[hbm] * 7,
        out_specs=[hbm, whole, hbm, hbm],
        scratch_shapes=[
            VMEM((2, 2, rows, n), BF16),
            VMEM((8, 128), jnp.int32),
            VMEM(catalog.shape, F32),
            VMEM(stations.shape, F32),
            VMEM((1, n), jnp.int32),
            VMEM((1, n), jnp.int32),
            VMEM((1, 4), F32),
            pltpu.SemaphoreType.DMA((8,)),
            VMEM((2, 2, rows, n), F32),
            VMEM((64, 1, 5 * CAP), F32),
            pltpu.SemaphoreType.DMA((3,)),
        ],
        name="front",
    )(
        visibilities,
        assignment.reshape(-1, 128),
        catalog,
        stations,
        input_order.reshape(1, n),
        station_flags.reshape(1, n),
        calibrator.reshape(1, 4),
    )

    far, own, place = pl.pallas_call(
        spread_kernel,
        out_shape=[shape(2, rows, n)] * 2 + [shape(8, n)],
        in_specs=[whole] * 2,
        out_specs=[whole] * 3,
        compiler_params=small,
        cost_estimate=pl.CostEstimate(flops=1 << 20, bytes_accessed=2 << 20, transcendentals=0),
        name="spread",
    )(visibilities, place)

    def turn(tile, s):
        return lax.ppermute(tile, "stn", ring(s))

    received = lax.all_to_all(send, "chan", 0, 0)
    tiles = [own, turn(ahead, 1), turn(far, 2), turn(behind, 3)]

    right_even, right_odd, left, model_own = pl.pallas_call(
        phasor_kernel,
        out_shape=[
            shape(chunks // 2, 4, n, 512, dtype=BF16),
            shape(chunks // 2, 4, n, 512, dtype=BF16),
            shape(chunks, 4, rows, 512, dtype=BF16),
            shape(2 * n, n),
        ],
        in_specs=[whole] * 2,
        out_specs=[whole, whole, hbm, whole],
        scratch_shapes=[
            VMEM((6, 16, 128), F32),
            VMEM((2, n, 128), F32),
            VMEM((8, 128), F32),
            [VMEM((4, n, 512), BF16)] * 2,
            [VMEM((6, 8, 256), F32)] * 2,
            pltpu.SemaphoreType.DMA((2,)),
        ],
        compiler_params=pltpu.CompilerParams(vmem_limit_bytes=8 << 20),
        cost_estimate=pl.CostEstimate(flops=10 << 30, bytes_accessed=21 << 20, transcendentals=0),
        name="phasor",
    )(received, place)

    solved = pl.pallas_call(
        solve_kernel,
        out_shape=shape(8, n),
        in_specs=[whole] * 6,
        out_specs=whole,
        scratch_shapes=[VMEM((n, n), F32)] * 3 + [VMEM((3, 8, n), F32), VMEM((3, n, 128), F32)],
        compiler_params=small,
        name="solve",
    )(model_own, *tiles, place)
    tables = [solved] + [lax.ppermute(solved, "stn", ring(s)) for s in (1, 2, 3)]

    model = pl.pallas_call(
        model_kernel,
        out_shape=shape(4, 2 * rows, n),
        in_specs=[whole] * 5,
        out_specs=whole,
        scratch_shapes=[VMEM((8, 128), F32)],
        compiler_params=small,
        cost_estimate=pl.CostEstimate(flops=4 << 30, bytes_accessed=21 << 20, transcendentals=0),
        name="model",
    )(right_even, right_odd, left, model_own, place)

    gains, residual, changes = pl.pallas_call(
        residual_kernel,
        grid=(4,),
        out_shape=[shape(2, 4, rows), shape(2, 4, rows, n, dtype=BF16), shape(ITERS, 4)],
        in_specs=[whole] * 7,
        out_specs=[
            pl.BlockSpec((2, 4, rows), lambda q: (0, 0, 0)),
            pl.BlockSpec((2, 1, rows, n), lambda q: (0, q, 0, 0)),
            pl.BlockSpec((ITERS, 4), lambda q: (0, 0)),
        ],
        scratch_shapes=[VMEM((4, 8, n), F32)],
        compiler_params=small,
        name="residual",
    )(model, visibilities, *tables, place)
    return (gains, residual, changes)


def solution(mesh):
    placed = (P(None, "chan", "stn", None), P("chan"), P(None, "chan"), P(), P(), P(), P())

    return jax.shard_map(
        per_device,
        mesh=mesh,
        in_specs=placed,
        out_specs=(P(None, "chan", "stn"), P(None, "chan", "stn", None), P(None, "chan")),
        check_vma=False,
    )
```

```python
import functools

import jax
import jax.numpy as jnp
from jax import lax
from jax.experimental import pallas as pl
from jax.experimental.pallas import tpu as pltpu
from jax.sharding import PartitionSpec as P


ITERS = 3
CAP = 32
VMEM = pltpu.VMEM
F32 = jnp.float32
BF16 = jnp.bfloat16
NT = (((1,), (1,)), ((), ()))

SIN_HALF = (3.141582005383235, -5.167142124470761, 2.541892570102862, -0.5546189642693115)
COS_HALF = (0.9999932847330446, -4.93393699910271, 4.041270253370243, -1.2220835776975139)
SIN_STEP = (1.9999932214850844, -0.33258196069982343)
COS_STEP = (1.999986449379199, -0.9969952843589359)


def horner(coefficients, x):
    total = coefficients[-1]
    for c in coefficients[-2::-1]:
        total = total * x + c
    return total


def split3(x):
    high = x.astype(BF16).astype(F32)
    rest = x - high
    middle = rest.astype(BF16).astype(F32)
    return high, middle, rest - middle


def spread_kernel(vis_ref, place_ref, *out_refs):
    k = lax.axis_index("stn")
    for s, out_ref in zip((1, 3, 0), out_refs):
        out_ref[...] = vis_ref[:, lax.rem(k + s, 4)].astype(F32)
    out_refs[3][...] = place_ref[...]


def front_kernel(
    vis_hbm, assign_hbm, cat_hbm, st_hbm, order_hbm, flag_hbm, cal_hbm, *refs
):
    send_hbm, place_ref, far_hbm, vis, own, cat, st, order, flag, cal, sem, wide, send, out_sem = refs
    c = lax.axis_index("chan")
    k = lax.axis_index("stn")
    copies = [
        pltpu.make_async_copy(source, target, sem.at[i])
        for i, (source, target) in enumerate(
            (
                (st_hbm, st),
                (order_hbm, order),
                (flag_hbm, flag),
                (assign_hbm.at[pl.ds(pl.multiple_of(c * 8, 8), 8)], own),
                (cat_hbm, cat),
                (vis_hbm.at[:, lax.rem(k + 2, 4)], vis),
                (cal_hbm, cal),
            )
        )
    ]
    for i in (5, 3, 4, 0, 1, 2, 6):
        copies[i].start()
    n = order.shape[1]
    copies[5].wait()
    wide[...] = vis[...].astype(F32)
    out = pltpu.make_async_copy(wide, far_hbm, out_sem.at[0])
    out.start()
    for copy in copies[3:5]:
        copy.wait()
    blocks = lax.broadcasted_iota(jnp.int32, (64, 128), 0)
    hits = [(blocks == own[t : t + 1]).astype(F32) for t in range(8)]
    stacked = jnp.concatenate(hits, axis=0).astype(BF16)
    upper = lax.broadcasted_iota(jnp.int32, (128, 128), 0) <= lax.broadcasted_iota(jnp.int32, (128, 128), 1)
    running = jnp.dot(stacked, upper.astype(F32).astype(BF16), preferred_element_type=F32)
    totals = jnp.dot(stacked, jnp.ones((128, 128), BF16), preferred_element_type=F32)
    before = jnp.full((64, 128), -1.0, F32)
    slot = lax.broadcasted_iota(jnp.int32, (CAP, 128), 0).astype(F32)
    pieces = split3(cat[...])
    left, right = [], []
    for t in range(8):
        part = slice(64 * t, 64 * t + 64)
        rank = jnp.sum(hits[t] * (running[part] + before), axis=0, keepdims=True)
        before = before + totals[part]
        chosen = slot == rank
        hit = hits[t].astype(BF16)
        for piece in pieces:
            left.append(hit)
            here = piece[:, 128 * t : 128 * t + 128]
            right.append(
                jnp.concatenate([jnp.where(chosen, here[f : f + 1], 0.0) for f in range(5)], axis=0).astype(BF16)
            )
    sent = lax.dot_general(
        jnp.concatenate(left, axis=1), jnp.concatenate(right, axis=1), NT, preferred_element_type=F32
    )
    send[:, 0, :] = sent
    sending = pltpu.make_async_copy(send, send_hbm, out_sem.at[1])
    sending.start()
    for copy in copies[:3] + copies[6:]:
        copy.wait()
    hot = (lax.broadcasted_iota(jnp.int32, (n, n), 0) == order[...]).astype(F32).astype(BF16)
    high, middle, low = split3(st[...])
    rows = jnp.concatenate([high, middle, low, flag[...].astype(F32), jnp.zeros((9, n), F32)], axis=0)
    placed = jnp.dot(rows.astype(BF16), hot, preferred_element_type=F32)
    middle_nu = 1.0 + (4.0 * c.astype(F32) + 1.5) * (1.0 / 512.0)
    place_ref[...] = jnp.zeros_like(place_ref)
    place_ref[0:1] = placed[6:7]
    for ch in range(4):
        place_ref[4 + ch : 5 + ch] = jnp.broadcast_to(cal[:, ch : ch + 1], (1, n))
    place_ref[1:2] = (placed[0:1] + placed[2:3] + placed[4:5]) * middle_nu
    place_ref[2:3] = (placed[1:2] + placed[3:4] + placed[5:6]) * middle_nu
    out.wait()
    sending.wait()


def phasor_kernel(
    recv_ref, place_ref, right_even, right_odd, left_out, model_ref, parts, spots, bright_rows, lefts, wides, sems
):
    rights = (right_even, right_odd)
    c = lax.axis_index("chan")
    k = lax.axis_index("stn")
    n = model_ref.shape[1]
    quarter = n // 4
    width = 256
    pairs = right_even.shape[0]
    tiles = width // 128
    base = 1.0 + 4.0 * c.astype(F32) * (1.0 / 512.0)
    middle_nu = 1.0 + (4.0 * c.astype(F32) + 1.5) * (1.0 / 512.0)
    step = jnp.full((8, width), 2.0 * jnp.pi / 1024.0, F32) / middle_nu
    sin1_by, sin3_by, cos2_by = SIN_STEP[0] * step, SIN_STEP[1] * step * step * step, COS_STEP[1] * step * step

    got = recv_ref[:, 0, :]
    got = jnp.concatenate([got, jnp.zeros((64, 256 - got.shape[1]), F32)], axis=1)
    got = jnp.concatenate([got, jnp.zeros((64, 256), F32)], axis=0).T
    lane = lax.broadcasted_iota(jnp.int32, (16, 128), 1)
    rows = []
    for f in range(5):
        low, high = got[32 * f : 32 * f + 16], got[32 * f + 16 : 32 * f + 32]
        rows.append(jnp.where(lane < 64, low, pltpu.roll(high, 64, 1)))
    parts[0] = rows[0]
    parts[1] = rows[1]
    for ch in range(4):
        log_nu = jnp.log(jnp.full((16, 128), 1.0, F32) * (base + ch / 512.0))
        parts[2 + ch] = rows[2] * jnp.exp(log_nu * (rows[3] + rows[4] * log_nu))

    for axis in range(2):
        for b in range(n // 128):
            row = place_ref[1 + axis : 2 + axis, 128 * b : 128 * b + 128]
            spots[axis, 128 * b : 128 * b + 128] = jnp.broadcast_to(row, (128, 128)).T

    def out_copy(chunk, buffer):
        return pltpu.make_async_copy(
            lefts[buffer].at[:, pl.ds(pl.multiple_of(k * quarter, quarter), quarter)],
            left_out.at[chunk],
            sems.at[buffer],
        )

    def phases(buffer, r0, g, channel):
        right, left, wide = rights[buffer].at[g], lefts[buffer], wides[buffer]
        rows = slice(r0, r0 + 8)
        x = jnp.concatenate([spots[0, rows]] * tiles, axis=1)
        y = jnp.concatenate([spots[1, rows]] * tiles, axis=1)
        turns = wide[0] * x + wide[1] * y
        r = turns - jnp.round(turns)
        t = r * r
        s = r * horner(SIN_HALF, t)
        h = horner(COS_HALF, t)
        half_cos = 0.5 - s * s
        half_sin = s * h
        square = turns * turns
        s2 = turns * (sin1_by + sin3_by * square)
        c2 = COS_STEP[0] + cos2_by * square
        twice = 2.0 - s2 * s2
        cc, ss = half_cos * c2, half_sin * s2
        sc, cs = half_sin * c2, half_cos * s2
        cos1, cos2 = cc + ss, cc - ss
        sin1, sin2 = sc - cs, sc + cs
        for ch, cosine, sine in (
            (1, cos1, sin1),
            (2, cos2, sin2),
            (0, twice * cos1 - cos2, twice * sin1 - sin2),
            (3, twice * cos2 - cos1, twice * sin2 - sin1),
        ):
            bright = wide[2 + ch]
            right[ch, rows, :width] = (bright * cosine).astype(BF16)
            right[ch, rows, width:] = (bright * sine).astype(BF16)
            if ch == channel or r0 // quarter == channel:
                left[ch, rows, :width] = cosine.astype(BF16)
                left[ch, rows, width:] = sine.astype(BF16)

    lefts[1][k] = jnp.zeros((n, 2 * width), BF16)
    right_odd[pairs - 1, k] = jnp.zeros((n, 2 * width), BF16)

    def chunks(*totals):
        def matmul(other, turn, block, g, own):
            left, right = lefts[other], rights[other].at[g]
            columns = slice(turn * width, turn * width + width)
            if block == 0:
                for half in range(2):
                    pltpu.matmul_push_rhs(
                        right[own, half * width : half * width + width, columns], turn, half, transpose=True
                    )
            rows = slice(128 * (block % 4), 128 * (block % 4) + 128)
            if block < 4:
                lhs = left[own, rows, columns]
            else:
                lhs = left[own, rows, (1 - turn) * width : (2 - turn) * width]
                if turn == 1:
                    lhs = -lhs
            for half in range(2):
                pltpu.matmul_acc_lhs(totals[8 * half + block], lhs, turn if block == 0 else None)

        def pair(channel, g, _):
            for sub in range(2):
                chunk = 2 * g + sub

                @pl.when(g > 0)
                def _():
                    out_copy(chunk - 2, sub).wait()

                for f in range(6):
                    for j in range(tiles):
                        row = parts[f, pl.ds(tiles * chunk + j, 1)]
                        wides[sub][f, :, 128 * j : 128 * j + 128] = jnp.broadcast_to(row, (8, 128))
                for turn in range(2):
                    for block in range(8):

                        def body(sub=sub, turn=turn, block=block):
                            matmul(1 - sub, turn, block, g if sub else lax.rem(g + pairs - 1, pairs), channel)
                            for i in range(4):
                                phases(sub, 32 * (8 * turn + block) + 8 * i, g, channel)

                        pl.when(g >= 0)(body)
                out_copy(chunk, sub).start()
            return 0

        for channel in range(4):

            @pl.when(k == channel)
            def _():
                lax.fori_loop(0, pairs, functools.partial(pair, channel), 0)

        for turn in range(2):
            for block in range(8):
                matmul(1, turn, block, pairs - 1, k)
        for sub in range(2):
            out_copy(2 * pairs - 2 + sub, sub).wait()
        bright_rows[0:4] = place_ref[4:8, :128]
        bright = bright_rows[pl.ds(k, 1)]
        bright = jnp.concatenate([bright, bright], axis=1)
        off = lax.broadcasted_iota(jnp.int32, (128, 128), 0) != lax.broadcasted_iota(jnp.int32, (128, 128), 1)
        for block in range(8):
            rows = slice(128 * block, 128 * block + 128)
            for half in range(2):
                total = pltpu.matmul_pop(totals[8 * half + block])
                if block < 4:
                    total = total + bright
                for j in range(2):
                    part = total[:, 128 * j : 128 * j + 128]
                    column = 2 * half + j
                    if column == block % 4:
                        part = jnp.where(off, part, 0.0)
                    model_ref[rows, 128 * column : 128 * column + 128] = part

    pl.run_scoped(chunks, *[pltpu.ACC(half)((128, 256), F32) for half in range(2) for _ in range(8)])


def model_kernel(right_even, right_odd, left_ref, own_ref, place_ref, model_ref, wide):
    k = lax.axis_index("stn")
    chunks, rows, half = left_ref.shape[0], left_ref.shape[2], left_ref.shape[3] // 2
    wide[0:4] = place_ref[4:8, :128]
    first = pl.multiple_of(k * rows, rows)
    model_ref[k, :rows] = own_ref[pl.ds(first, rows)]
    model_ref[k, rows:] = own_ref[pl.ds(4 * rows + first, rows)]

    def channel(i, _):
        ch = lax.rem(k + 1 + i, 4)
        lefts = []
        for q in range(chunks):
            left = left_ref[q, ch]
            cosine, sine = left[:, :half], left[:, half:]
            lefts.append(jnp.concatenate([left, jnp.concatenate([sine, -cosine], axis=1)], axis=0))
        total = lax.dot_general(
            jnp.concatenate(lefts, axis=1),
            jnp.concatenate([(right_even, right_odd)[q % 2][q // 2, ch] for q in range(chunks)], axis=1),
            NT,
            preferred_element_type=F32,
        )
        bright = jnp.concatenate([wide[pl.ds(ch, 1)]] * 4, axis=1)
        model_ref[ch, :rows] = total[:rows] + bright
        model_ref[ch, rows:] = total[rows:]
        return 0

    lax.fori_loop(0, 3, channel, 0)


def solve_kernel(model_ref, v0, v1, v2, v3, ok_ref, out_ref, a_re, a_im, b_ab, wide, part):
    k = lax.axis_index("stn")
    n = v0.shape[2]
    quarter = n // 4
    ok = ok_ref[0:1]

    def fold(x):
        return (x[:, :128] + x[:, 128:256]) + (x[:, 256:384] + x[:, 384:])

    def set_up(s, v):
        first = lax.rem(k + 4 - s, 4) * quarter

        def body(i, _):
            local = pl.multiple_of(8 * i, 8)
            r0 = pl.multiple_of(first + 8 * i, 8)
            mr = model_ref[pl.ds(r0, 8)]
            mi = model_ref[pl.ds(n + r0, 8)]
            vr = v[0, pl.ds(local, 8)]
            vi = v[1, pl.ds(local, 8)]
            ar = mr * vr + mi * vi
            ai = mr * vi - mi * vr
            b = mr * mr + mi * mi
            a_re[pl.ds(r0, 8)] = ar
            a_im[pl.ds(r0, 8)] = ai
            b_ab[pl.ds(r0, 8)] = b
            g = wide[0]
            part[0, pl.ds(r0, 8)] = fold(ar * g)
            part[1, pl.ds(r0, 8)] = fold(ai * g)
            part[2, pl.ds(r0, 8)] = fold(b * g)
            return 0

        lax.fori_loop(0, quarter // 8, body, 0, unroll=4)

    def sums():
        gr, gi, gg = wide[0], wide[1], wide[2]

        def body(i, _):
            r0 = pl.multiple_of(8 * i, 8)
            ar, ai = a_re[pl.ds(r0, 8)], a_im[pl.ds(r0, 8)]
            part[0, pl.ds(r0, 8)] = fold(ar * gr - ai * gi)
            part[1, pl.ds(r0, 8)] = fold(ar * gi + ai * gr)
            part[2, pl.ds(r0, 8)] = fold(b_ab[pl.ds(r0, 8)] * gg)
            return 0

        lax.fori_loop(0, n // 8, body, 0, unroll=4)

    def total(q):
        return jnp.concatenate(
            [jnp.sum(part[q, 128 * b : 128 * b + 128].T, axis=0, keepdims=True) for b in range(n // 128)], axis=1
        )

    g_re, g_im = jnp.ones((1, n), F32), jnp.zeros((1, n), F32)
    out_ref[...] = jnp.zeros_like(out_ref)
    for iteration in range(ITERS):
        wide[0] = jnp.broadcast_to(ok * g_re, (8, n))
        wide[1] = jnp.broadcast_to(ok * g_im, (8, n))
        wide[2] = jnp.broadcast_to(ok * (g_re * g_re + g_im * g_im), (8, n))
        if iteration == 0:
            for s, v in enumerate((v0, v1, v2, v3)):
                set_up(s, v)
        else:
            sums()
        below = total(2) * ok + 1e-6 + (1.0 - ok)
        new_re = total(0) * ok / below
        new_im = total(1) * ok / below
        if iteration % 2 == 1:
            new_re = 0.5 * (new_re + g_re)
            new_im = 0.5 * (new_im + g_im)
        moved = jnp.sum((new_re - g_re) ** 2 + (new_im - g_im) ** 2, axis=1, keepdims=True)
        size = jnp.sum(new_re * new_re + new_im * new_im, axis=1, keepdims=True)
        out_ref[2 + iteration : 3 + iteration] = jnp.broadcast_to(moved / (size + 1e-6), (1, n))
        g_re, g_im = new_re, new_im
    out_ref[0:1] = g_re
    out_ref[1:2] = g_im


def residual_kernel(model_ref, vis_ref, g0, g1, g2, g3, ok_ref, gains_ref, res_ref, change_ref, table):
    k = lax.axis_index("stn")
    ch = pl.program_id(0)
    n = vis_ref.shape[3]
    quarter = n // 4
    lanes = pl.ds(pl.multiple_of(k * quarter, 128), quarter)

    @pl.when(ch == 0)
    def _():
        for s, g in enumerate((g0, g1, g2, g3)):
            table[lax.rem(k + 4 - s, 4)] = g[...]
        lane = lax.broadcasted_iota(jnp.int32, (ITERS, 4), 1)
        history = jnp.zeros((ITERS, 4), F32)
        for q in range(4):
            gains_ref[0, q : q + 1] = table[q, 0:1, lanes]
            gains_ref[1, q : q + 1] = table[q, 1:2, lanes]
            history = jnp.where(lane == q, table[q, 2 : 2 + ITERS, 0:4], history)
        change_ref[...] = history

    def column(row):
        return jnp.broadcast_to(row, (128, 128)).T

    gi_re = column(table[ch, 0:1, lanes])
    gi_im = column(table[ch, 1:2, lanes])
    ui = column(ok_ref[0:1, lanes])
    columns = lax.broadcasted_iota(jnp.int32, (16, 128), 1)
    sub = lax.broadcasted_iota(jnp.int32, (16, 128), 0)
    gj_re = [jnp.broadcast_to(table[ch, 0:1, 128 * b : 128 * b + 128], (16, 128)) for b in range(4)]
    gj_im = [jnp.broadcast_to(table[ch, 1:2, 128 * b : 128 * b + 128], (16, 128)) for b in range(4)]
    uj = [jnp.broadcast_to(ok_ref[0:1, 128 * b : 128 * b + 128], (16, 128)) for b in range(4)]
    for i in range(quarter // 16):
        rows = slice(16 * i, 16 * i + 16)
        a_re, a_im, a_ok = gi_re[rows], gi_im[rows], ui[rows]
        for b in range(4):
            at = slice(128 * b, 128 * b + 128)
            off = columns + 128 * b != sub + (k * quarter + 16 * i)
            e = jnp.where(off, a_ok * uj[b], 0.0)
            p_re = a_re * gj_re[b] + a_im * gj_im[b]
            p_im = a_im * gj_re[b] - a_re * gj_im[b]
            mr = model_ref[ch, rows, at]
            mi = model_ref[ch, slice(quarter + 16 * i, quarter + 16 * i + 16), at]
            vr = vis_ref[0, ch, rows, at].astype(F32)
            vi = vis_ref[1, ch, rows, at].astype(F32)
            res_ref[0, 0, rows, at] = (e * (vr - (p_re * mr - p_im * mi))).astype(BF16)
            res_ref[1, 0, rows, at] = (e * (vi - (p_re * mi + p_im * mr))).astype(BF16)


def per_device(visibilities, calibrator, catalog, assignment, stations, input_order, station_flags):
    rows, n = visibilities.shape[2], visibilities.shape[3]
    sources = 64 * CAP
    chunks = sources // 256
    whole = pl.BlockSpec(memory_space=VMEM)
    hbm = pl.BlockSpec(memory_space=pltpu.HBM)
    small = pltpu.CompilerParams(vmem_limit_bytes=6 << 20)

    def shape(*dims, dtype=F32):
        return jax.ShapeDtypeStruct(dims, dtype)

    def ring(s):
        return [(i, (i + s) % 4) for i in range(4)]

    send, place, far = pl.pallas_call(
        front_kernel,
        out_shape=[shape(64, 1, 5 * CAP), shape(8, n), shape(2, rows, n)],
        in_specs=[hbm] * 7,
        out_specs=[hbm, whole, hbm],
        scratch_shapes=[
            VMEM((2, rows, n), BF16),
            VMEM((8, 128), jnp.int32),
            VMEM(catalog.shape, F32),
            VMEM(stations.shape, F32),
            VMEM((1, n), jnp.int32),
            VMEM((1, n), jnp.int32),
            VMEM((1, 4), F32),
            pltpu.SemaphoreType.DMA((7,)),
            VMEM((2, rows, n), F32),
            VMEM((64, 1, 5 * CAP), F32),
            pltpu.SemaphoreType.DMA((2,)),
        ],
        name="front",
    )(
        visibilities,
        assignment.reshape(-1, 128),
        catalog,
        stations,
        input_order.reshape(1, n),
        station_flags.reshape(1, n),
        calibrator.reshape(1, 4),
    )

    ahead, behind, own, place = pl.pallas_call(
        spread_kernel,
        out_shape=[shape(2, rows, n)] * 3 + [shape(8, n)],
        in_specs=[whole] * 2,
        out_specs=[whole] * 4,
        compiler_params=small,
        cost_estimate=pl.CostEstimate(flops=1 << 20, bytes_accessed=2 << 20, transcendentals=0),
        name="spread",
    )(visibilities, place)

    def turn(tile, s):
        return lax.ppermute(tile, "stn", ring(s))

    received = lax.all_to_all(send, "chan", 0, 0)
    tiles = [own, turn(ahead, 1), turn(far, 2), turn(behind, 3)]

    right_even, right_odd, left, model_own = pl.pallas_call(
        phasor_kernel,
        out_shape=[
            shape(chunks // 2, 4, n, 512, dtype=BF16),
            shape(chunks // 2, 4, n, 512, dtype=BF16),
            shape(chunks, 4, rows, 512, dtype=BF16),
            shape(2 * n, n),
        ],
        in_specs=[whole] * 2,
        out_specs=[whole, whole, hbm, whole],
        scratch_shapes=[
            VMEM((6, 16, 128), F32),
            VMEM((2, n, 128), F32),
            VMEM((8, 128), F32),
            [VMEM((4, n, 512), BF16)] * 2,
            [VMEM((6, 8, 256), F32)] * 2,
            pltpu.SemaphoreType.DMA((2,)),
        ],
        compiler_params=pltpu.CompilerParams(vmem_limit_bytes=8 << 20),
        cost_estimate=pl.CostEstimate(flops=10 << 30, bytes_accessed=21 << 20, transcendentals=0),
        name="phasor",
    )(received, place)

    solved = pl.pallas_call(
        solve_kernel,
        out_shape=shape(8, n),
        in_specs=[whole] * 6,
        out_specs=whole,
        scratch_shapes=[VMEM((n, n), F32)] * 3 + [VMEM((3, 8, n), F32), VMEM((3, n, 128), F32)],
        compiler_params=small,
        name="solve",
    )(model_own, *tiles, place)
    tables = [solved] + [lax.ppermute(solved, "stn", ring(s)) for s in (1, 2, 3)]

    model = pl.pallas_call(
        model_kernel,
        out_shape=shape(4, 2 * rows, n),
        in_specs=[whole] * 5,
        out_specs=whole,
        scratch_shapes=[VMEM((8, 128), F32)],
        compiler_params=small,
        cost_estimate=pl.CostEstimate(flops=4 << 30, bytes_accessed=21 << 20, transcendentals=0),
        name="model",
    )(right_even, right_odd, left, model_own, place)

    gains, residual, changes = pl.pallas_call(
        residual_kernel,
        grid=(4,),
        out_shape=[shape(2, 4, rows), shape(2, 4, rows, n, dtype=BF16), shape(ITERS, 4)],
        in_specs=[whole] * 7,
        out_specs=[
            pl.BlockSpec((2, 4, rows), lambda q: (0, 0, 0)),
            pl.BlockSpec((2, 1, rows, n), lambda q: (0, q, 0, 0)),
            pl.BlockSpec((ITERS, 4), lambda q: (0, 0)),
        ],
        scratch_shapes=[VMEM((4, 8, n), F32)],
        compiler_params=small,
        name="residual",
    )(model, visibilities, *tables, place)
    return (gains, residual, changes)


def solution(mesh):
    placed = (P(None, "chan", "stn", None), P("chan"), P(None, "chan"), P(), P(), P(), P())

    return jax.shard_map(
        per_device,
        mesh=mesh,
        in_specs=placed,
        out_specs=(P(None, "chan", "stn"), P(None, "chan", "stn", None), P(None, "chan")),
        check_vma=False,
    )
```

```python
import functools

import jax
import jax.numpy as jnp
from jax import lax
from jax.experimental import pallas as pl
from jax.experimental.pallas import tpu as pltpu
from jax.sharding import PartitionSpec as P


ITERS = 3
CAP = 32
VMEM = pltpu.VMEM
F32 = jnp.float32
BF16 = jnp.bfloat16
NT = (((1,), (1,)), ((), ()))

SIN_HALF = (3.141582005383235, -5.167142124470761, 2.541892570102862, -0.5546189642693115)
COS_HALF = (0.9999932847330446, -4.93393699910271, 4.041270253370243, -1.2220835776975139)
SIN_STEP = (1.9999932214850844, -0.33258196069982343)
COS_STEP = (1.999986449379199, -0.9969952843589359)


def horner(coefficients, x):
    total = coefficients[-1]
    for c in coefficients[-2::-1]:
        total = total * x + c
    return total


def split3(x):
    high = x.astype(BF16).astype(F32)
    rest = x - high
    middle = rest.astype(BF16).astype(F32)
    return high, middle, rest - middle


def spread_kernel(vis_ref, place_ref, *out_refs):
    k = lax.axis_index("stn")
    for s, out_ref in zip((1, 3, 0), out_refs):
        out_ref[...] = vis_ref[:, lax.rem(k + s, 4)].astype(F32)
    out_refs[3][...] = place_ref[...]


def front_kernel(
    vis_hbm, assign_hbm, cat_hbm, st_hbm, order_hbm, flag_hbm, cal_hbm, *refs
):
    send_ref, place_ref, far_hbm, vis, own, cat, st, order, flag, cal, sem, wide, out_sem = refs
    c = lax.axis_index("chan")
    k = lax.axis_index("stn")
    copies = [
        pltpu.make_async_copy(source, target, sem.at[i])
        for i, (source, target) in enumerate(
            (
                (st_hbm, st),
                (order_hbm, order),
                (flag_hbm, flag),
                (assign_hbm.at[pl.ds(pl.multiple_of(c * 8, 8), 8)], own),
                (cat_hbm, cat),
                (vis_hbm.at[:, lax.rem(k + 2, 4)], vis),
                (cal_hbm, cal),
            )
        )
    ]
    for copy in copies:
        copy.start()
    n = order.shape[1]
    for copy in copies[:3] + copies[6:]:
        copy.wait()
    hot = (lax.broadcasted_iota(jnp.int32, (n, n), 0) == order[...]).astype(F32).astype(BF16)
    high, middle, low = split3(st[...])
    rows = jnp.concatenate([high, middle, low, flag[...].astype(F32), jnp.zeros((9, n), F32)], axis=0)
    placed = jnp.dot(rows.astype(BF16), hot, preferred_element_type=F32)
    middle_nu = 1.0 + (4.0 * c.astype(F32) + 1.5) * (1.0 / 512.0)
    place_ref[...] = jnp.zeros_like(place_ref)
    place_ref[0:1] = placed[6:7]
    for ch in range(4):
        place_ref[4 + ch : 5 + ch] = jnp.broadcast_to(cal[:, ch : ch + 1], (1, n))
    place_ref[1:2] = (placed[0:1] + placed[2:3] + placed[4:5]) * middle_nu
    place_ref[2:3] = (placed[1:2] + placed[3:4] + placed[5:6]) * middle_nu
    copies[5].wait()
    wide[...] = vis[...].astype(F32)
    out = pltpu.make_async_copy(wide, far_hbm, out_sem)
    out.start()
    for copy in copies[3:5]:
        copy.wait()
    blocks = lax.broadcasted_iota(jnp.int32, (64, 128), 0)
    hits = [(blocks == own[t : t + 1]).astype(F32) for t in range(8)]
    stacked = jnp.concatenate(hits, axis=0).astype(BF16)
    upper = lax.broadcasted_iota(jnp.int32, (128, 128), 0) <= lax.broadcasted_iota(jnp.int32, (128, 128), 1)
    running = jnp.dot(stacked, upper.astype(F32).astype(BF16), preferred_element_type=F32)
    totals = jnp.dot(stacked, jnp.ones((128, 128), BF16), preferred_element_type=F32)
    before = jnp.full((64, 128), -1.0, F32)
    slot = lax.broadcasted_iota(jnp.int32, (CAP, 128), 0).astype(F32)
    pieces = split3(cat[...])
    left, right = [], []
    for t in range(8):
        part = slice(64 * t, 64 * t + 64)
        rank = jnp.sum(hits[t] * (running[part] + before), axis=0, keepdims=True)
        before = before + totals[part]
        chosen = slot == rank
        hit = hits[t].astype(BF16)
        for piece in pieces:
            left.append(hit)
            here = piece[:, 128 * t : 128 * t + 128]
            right.append(
                jnp.concatenate([jnp.where(chosen, here[f : f + 1], 0.0) for f in range(5)], axis=0).astype(BF16)
            )
    sent = lax.dot_general(
        jnp.concatenate(left, axis=1), jnp.concatenate(right, axis=1), NT, preferred_element_type=F32
    )
    send_ref[:, 0, :] = sent
    out.wait()


def phasor_kernel(
    recv_ref, place_ref, right_even, right_odd, left_out, model_ref, parts, spots, bright_rows, lefts, wides, sems
):
    rights = (right_even, right_odd)
    c = lax.axis_index("chan")
    k = lax.axis_index("stn")
    n = model_ref.shape[1]
    quarter = n // 4
    width = 256
    pairs = right_even.shape[0]
    tiles = width // 128
    base = 1.0 + 4.0 * c.astype(F32) * (1.0 / 512.0)
    middle_nu = 1.0 + (4.0 * c.astype(F32) + 1.5) * (1.0 / 512.0)
    step = jnp.full((8, width), 2.0 * jnp.pi / 1024.0, F32) / middle_nu
    sin1_by, sin3_by, cos2_by = SIN_STEP[0] * step, SIN_STEP[1] * step * step * step, COS_STEP[1] * step * step

    got = recv_ref[:, 0, :]
    got = jnp.concatenate([got, jnp.zeros((64, 256 - got.shape[1]), F32)], axis=1)
    got = jnp.concatenate([got, jnp.zeros((64, 256), F32)], axis=0).T
    lane = lax.broadcasted_iota(jnp.int32, (16, 128), 1)
    rows = []
    for f in range(5):
        low, high = got[32 * f : 32 * f + 16], got[32 * f + 16 : 32 * f + 32]
        rows.append(jnp.where(lane < 64, low, pltpu.roll(high, 64, 1)))
    parts[0] = rows[0]
    parts[1] = rows[1]
    for ch in range(4):
        log_nu = jnp.log(jnp.full((16, 128), 1.0, F32) * (base + ch / 512.0))
        parts[2 + ch] = rows[2] * jnp.exp(log_nu * (rows[3] + rows[4] * log_nu))

    for axis in range(2):
        for b in range(n // 128):
            row = place_ref[1 + axis : 2 + axis, 128 * b : 128 * b + 128]
            spots[axis, 128 * b : 128 * b + 128] = jnp.broadcast_to(row, (128, 128)).T

    def out_copy(chunk, buffer):
        return pltpu.make_async_copy(
            lefts[buffer].at[:, pl.ds(pl.multiple_of(k * quarter, quarter), quarter)],
            left_out.at[chunk],
            sems.at[buffer],
        )

    def phases(buffer, r0, g, channel):
        right, left, wide = rights[buffer].at[g], lefts[buffer], wides[buffer]
        rows = slice(r0, r0 + 8)
        x = jnp.concatenate([spots[0, rows]] * tiles, axis=1)
        y = jnp.concatenate([spots[1, rows]] * tiles, axis=1)
        turns = wide[0] * x + wide[1] * y
        r = turns - jnp.round(turns)
        t = r * r
        s = r * horner(SIN_HALF, t)
        h = horner(COS_HALF, t)
        half_cos = 0.5 - s * s
        half_sin = s * h
        square = turns * turns
        s2 = turns * (sin1_by + sin3_by * square)
        c2 = COS_STEP[0] + cos2_by * square
        twice = 2.0 - s2 * s2
        cc, ss = half_cos * c2, half_sin * s2
        sc, cs = half_sin * c2, half_cos * s2
        cos1, cos2 = cc + ss, cc - ss
        sin1, sin2 = sc - cs, sc + cs
        for ch, cosine, sine in (
            (1, cos1, sin1),
            (2, cos2, sin2),
            (0, twice * cos1 - cos2, twice * sin1 - sin2),
            (3, twice * cos2 - cos1, twice * sin2 - sin1),
        ):
            bright = wide[2 + ch]
            right[ch, rows, :width] = (bright * cosine).astype(BF16)
            right[ch, rows, width:] = (bright * sine).astype(BF16)
            if ch == channel or r0 // quarter == channel:
                left[ch, rows, :width] = cosine.astype(BF16)
                left[ch, rows, width:] = sine.astype(BF16)

    lefts[1][k] = jnp.zeros((n, 2 * width), BF16)
    right_odd[pairs - 1, k] = jnp.zeros((n, 2 * width), BF16)

    def chunks(*totals):
        def matmul(other, turn, block, g, own):
            left, right = lefts[other], rights[other].at[g]
            columns = slice(turn * width, turn * width + width)
            if block == 0:
                for half in range(2):
                    pltpu.matmul_push_rhs(
                        right[own, half * width : half * width + width, columns], turn, half, transpose=True
                    )
            rows = slice(128 * (block % 4), 128 * (block % 4) + 128)
            if block < 4:
                lhs = left[own, rows, columns]
            else:
                lhs = left[own, rows, (1 - turn) * width : (2 - turn) * width]
                if turn == 1:
                    lhs = -lhs
            for half in range(2):
                pltpu.matmul_acc_lhs(totals[8 * half + block], lhs, turn if block == 0 else None)

        def pair(channel, g, _):
            for sub in range(2):
                chunk = 2 * g + sub

                @pl.when(g > 0)
                def _():
                    out_copy(chunk - 2, sub).wait()

                for f in range(6):
                    for j in range(tiles):
                        row = parts[f, pl.ds(tiles * chunk + j, 1)]
                        wides[sub][f, :, 128 * j : 128 * j + 128] = jnp.broadcast_to(row, (8, 128))
                for turn in range(2):
                    for block in range(8):

                        def body(sub=sub, turn=turn, block=block):
                            matmul(1 - sub, turn, block, g if sub else lax.rem(g + pairs - 1, pairs), channel)
                            for i in range(4):
                                phases(sub, 32 * (8 * turn + block) + 8 * i, g, channel)

                        pl.when(g >= 0)(body)
                out_copy(chunk, sub).start()
            return 0

        for channel in range(4):

            @pl.when(k == channel)
            def _():
                lax.fori_loop(0, pairs, functools.partial(pair, channel), 0)

        for turn in range(2):
            for block in range(8):
                matmul(1, turn, block, pairs - 1, k)
        for sub in range(2):
            out_copy(2 * pairs - 2 + sub, sub).wait()
        bright_rows[0:4] = place_ref[4:8, :128]
        bright = bright_rows[pl.ds(k, 1)]
        bright = jnp.concatenate([bright, bright], axis=1)
        off = lax.broadcasted_iota(jnp.int32, (128, 128), 0) != lax.broadcasted_iota(jnp.int32, (128, 128), 1)
        for block in range(8):
            rows = slice(128 * block, 128 * block + 128)
            for half in range(2):
                total = pltpu.matmul_pop(totals[8 * half + block])
                if block < 4:
                    total = total + bright
                for j in range(2):
                    part = total[:, 128 * j : 128 * j + 128]
                    column = 2 * half + j
                    if column == block % 4:
                        part = jnp.where(off, part, 0.0)
                    model_ref[rows, 128 * column : 128 * column + 128] = part

    pl.run_scoped(chunks, *[pltpu.ACC(half)((128, 256), F32) for half in range(2) for _ in range(8)])


def model_kernel(right_even, right_odd, left_ref, own_ref, place_ref, model_ref, wide):
    k = lax.axis_index("stn")
    chunks, rows, half = left_ref.shape[0], left_ref.shape[2], left_ref.shape[3] // 2
    wide[0:4] = place_ref[4:8, :128]
    first = pl.multiple_of(k * rows, rows)
    model_ref[k, :rows] = own_ref[pl.ds(first, rows)]
    model_ref[k, rows:] = own_ref[pl.ds(4 * rows + first, rows)]

    def channel(i, _):
        ch = lax.rem(k + 1 + i, 4)
        lefts = []
        for q in range(chunks):
            left = left_ref[q, ch]
            cosine, sine = left[:, :half], left[:, half:]
            lefts.append(jnp.concatenate([left, jnp.concatenate([sine, -cosine], axis=1)], axis=0))
        total = lax.dot_general(
            jnp.concatenate(lefts, axis=1),
            jnp.concatenate([(right_even, right_odd)[q % 2][q // 2, ch] for q in range(chunks)], axis=1),
            NT,
            preferred_element_type=F32,
        )
        bright = jnp.concatenate([wide[pl.ds(ch, 1)]] * 4, axis=1)
        model_ref[ch, :rows] = total[:rows] + bright
        model_ref[ch, rows:] = total[rows:]
        return 0

    lax.fori_loop(0, 3, channel, 0)


def solve_kernel(model_ref, v0, v1, v2, v3, ok_ref, out_ref, a_re, a_im, b_ab, wide, part):
    k = lax.axis_index("stn")
    n = v0.shape[2]
    quarter = n // 4
    ok = ok_ref[0:1]

    def fold(x):
        return (x[:, :128] + x[:, 128:256]) + (x[:, 256:384] + x[:, 384:])

    def set_up(s, v):
        first = lax.rem(k + 4 - s, 4) * quarter

        def body(i, _):
            local = pl.multiple_of(8 * i, 8)
            r0 = pl.multiple_of(first + 8 * i, 8)
            mr = model_ref[pl.ds(r0, 8)]
            mi = model_ref[pl.ds(n + r0, 8)]
            vr = v[0, pl.ds(local, 8)]
            vi = v[1, pl.ds(local, 8)]
            ar = mr * vr + mi * vi
            ai = mr * vi - mi * vr
            b = mr * mr + mi * mi
            a_re[pl.ds(r0, 8)] = ar
            a_im[pl.ds(r0, 8)] = ai
            b_ab[pl.ds(r0, 8)] = b
            g = wide[0]
            part[0, pl.ds(r0, 8)] = fold(ar * g)
            part[1, pl.ds(r0, 8)] = fold(ai * g)
            part[2, pl.ds(r0, 8)] = fold(b * g)
            return 0

        lax.fori_loop(0, quarter // 8, body, 0, unroll=4)

    def sums():
        gr, gi, gg = wide[0], wide[1], wide[2]

        def body(i, _):
            r0 = pl.multiple_of(8 * i, 8)
            ar, ai = a_re[pl.ds(r0, 8)], a_im[pl.ds(r0, 8)]
            part[0, pl.ds(r0, 8)] = fold(ar * gr - ai * gi)
            part[1, pl.ds(r0, 8)] = fold(ar * gi + ai * gr)
            part[2, pl.ds(r0, 8)] = fold(b_ab[pl.ds(r0, 8)] * gg)
            return 0

        lax.fori_loop(0, n // 8, body, 0, unroll=4)

    def total(q):
        return jnp.concatenate(
            [jnp.sum(part[q, 128 * b : 128 * b + 128].T, axis=0, keepdims=True) for b in range(n // 128)], axis=1
        )

    g_re, g_im = jnp.ones((1, n), F32), jnp.zeros((1, n), F32)
    out_ref[...] = jnp.zeros_like(out_ref)
    for iteration in range(ITERS):
        wide[0] = jnp.broadcast_to(ok * g_re, (8, n))
        wide[1] = jnp.broadcast_to(ok * g_im, (8, n))
        wide[2] = jnp.broadcast_to(ok * (g_re * g_re + g_im * g_im), (8, n))
        if iteration == 0:
            for s, v in enumerate((v0, v1, v2, v3)):
                set_up(s, v)
        else:
            sums()
        below = total(2) * ok + 1e-6 + (1.0 - ok)
        new_re = total(0) * ok / below
        new_im = total(1) * ok / below
        if iteration % 2 == 1:
            new_re = 0.5 * (new_re + g_re)
            new_im = 0.5 * (new_im + g_im)
        moved = jnp.sum((new_re - g_re) ** 2 + (new_im - g_im) ** 2, axis=1, keepdims=True)
        size = jnp.sum(new_re * new_re + new_im * new_im, axis=1, keepdims=True)
        out_ref[2 + iteration : 3 + iteration] = jnp.broadcast_to(moved / (size + 1e-6), (1, n))
        g_re, g_im = new_re, new_im
    out_ref[0:1] = g_re
    out_ref[1:2] = g_im


def residual_kernel(model_ref, vis_ref, g0, g1, g2, g3, ok_ref, gains_ref, res_ref, change_ref, table):
    k = lax.axis_index("stn")
    ch = pl.program_id(0)
    n = vis_ref.shape[3]
    quarter = n // 4
    lanes = pl.ds(pl.multiple_of(k * quarter, 128), quarter)

    @pl.when(ch == 0)
    def _():
        for s, g in enumerate((g0, g1, g2, g3)):
            table[lax.rem(k + 4 - s, 4)] = g[...]
        lane = lax.broadcasted_iota(jnp.int32, (ITERS, 4), 1)
        history = jnp.zeros((ITERS, 4), F32)
        for q in range(4):
            gains_ref[0, q : q + 1] = table[q, 0:1, lanes]
            gains_ref[1, q : q + 1] = table[q, 1:2, lanes]
            history = jnp.where(lane == q, table[q, 2 : 2 + ITERS, 0:4], history)
        change_ref[...] = history

    def column(row):
        return jnp.broadcast_to(row, (128, 128)).T

    gi_re = column(table[ch, 0:1, lanes])
    gi_im = column(table[ch, 1:2, lanes])
    ui = column(ok_ref[0:1, lanes])
    columns = lax.broadcasted_iota(jnp.int32, (16, 128), 1)
    sub = lax.broadcasted_iota(jnp.int32, (16, 128), 0)
    gj_re = [jnp.broadcast_to(table[ch, 0:1, 128 * b : 128 * b + 128], (16, 128)) for b in range(4)]
    gj_im = [jnp.broadcast_to(table[ch, 1:2, 128 * b : 128 * b + 128], (16, 128)) for b in range(4)]
    uj = [jnp.broadcast_to(ok_ref[0:1, 128 * b : 128 * b + 128], (16, 128)) for b in range(4)]
    for i in range(quarter // 16):
        rows = slice(16 * i, 16 * i + 16)
        a_re, a_im, a_ok = gi_re[rows], gi_im[rows], ui[rows]
        for b in range(4):
            at = slice(128 * b, 128 * b + 128)
            off = columns + 128 * b != sub + (k * quarter + 16 * i)
            e = jnp.where(off, a_ok * uj[b], 0.0)
            p_re = a_re * gj_re[b] + a_im * gj_im[b]
            p_im = a_im * gj_re[b] - a_re * gj_im[b]
            mr = model_ref[ch, rows, at]
            mi = model_ref[ch, slice(quarter + 16 * i, quarter + 16 * i + 16), at]
            vr = vis_ref[0, ch, rows, at].astype(F32)
            vi = vis_ref[1, ch, rows, at].astype(F32)
            res_ref[0, 0, rows, at] = (e * (vr - (p_re * mr - p_im * mi))).astype(BF16)
            res_ref[1, 0, rows, at] = (e * (vi - (p_re * mi + p_im * mr))).astype(BF16)


def per_device(visibilities, calibrator, catalog, assignment, stations, input_order, station_flags):
    rows, n = visibilities.shape[2], visibilities.shape[3]
    sources = 64 * CAP
    chunks = sources // 256
    whole = pl.BlockSpec(memory_space=VMEM)
    hbm = pl.BlockSpec(memory_space=pltpu.HBM)
    small = pltpu.CompilerParams(vmem_limit_bytes=6 << 20)

    def shape(*dims, dtype=F32):
        return jax.ShapeDtypeStruct(dims, dtype)

    def ring(s):
        return [(i, (i + s) % 4) for i in range(4)]

    send, place, far = pl.pallas_call(
        front_kernel,
        out_shape=[shape(64, 1, 5 * CAP), shape(8, n), shape(2, rows, n)],
        in_specs=[hbm] * 7,
        out_specs=[whole] * 2 + [hbm],
        scratch_shapes=[
            VMEM((2, rows, n), BF16),
            VMEM((8, 128), jnp.int32),
            VMEM(catalog.shape, F32),
            VMEM(stations.shape, F32),
            VMEM((1, n), jnp.int32),
            VMEM((1, n), jnp.int32),
            VMEM((1, 4), F32),
            pltpu.SemaphoreType.DMA((7,)),
            VMEM((2, rows, n), F32),
            pltpu.SemaphoreType.DMA,
        ],
        name="front",
    )(
        visibilities,
        assignment.reshape(-1, 128),
        catalog,
        stations,
        input_order.reshape(1, n),
        station_flags.reshape(1, n),
        calibrator.reshape(1, 4),
    )

    ahead, behind, own, place = pl.pallas_call(
        spread_kernel,
        out_shape=[shape(2, rows, n)] * 3 + [shape(8, n)],
        in_specs=[whole] * 2,
        out_specs=[whole] * 4,
        compiler_params=small,
        cost_estimate=pl.CostEstimate(flops=1 << 20, bytes_accessed=2 << 20, transcendentals=0),
        name="spread",
    )(visibilities, place)

    def turn(tile, s):
        return lax.ppermute(tile, "stn", ring(s))

    received = lax.all_to_all(send, "chan", 0, 0)
    tiles = [own, turn(ahead, 1), turn(far, 2), turn(behind, 3)]

    right_even, right_odd, left, model_own = pl.pallas_call(
        phasor_kernel,
        out_shape=[
            shape(chunks // 2, 4, n, 512, dtype=BF16),
            shape(chunks // 2, 4, n, 512, dtype=BF16),
            shape(chunks, 4, rows, 512, dtype=BF16),
            shape(2 * n, n),
        ],
        in_specs=[whole] * 2,
        out_specs=[whole, whole, hbm, whole],
        scratch_shapes=[
            VMEM((6, 16, 128), F32),
            VMEM((2, n, 128), F32),
            VMEM((8, 128), F32),
            [VMEM((4, n, 512), BF16)] * 2,
            [VMEM((6, 8, 256), F32)] * 2,
            pltpu.SemaphoreType.DMA((2,)),
        ],
        compiler_params=pltpu.CompilerParams(vmem_limit_bytes=8 << 20),
        cost_estimate=pl.CostEstimate(flops=10 << 30, bytes_accessed=21 << 20, transcendentals=0),
        name="phasor",
    )(received, place)

    solved = pl.pallas_call(
        solve_kernel,
        out_shape=shape(8, n),
        in_specs=[whole] * 6,
        out_specs=whole,
        scratch_shapes=[VMEM((n, n), F32)] * 3 + [VMEM((3, 8, n), F32), VMEM((3, n, 128), F32)],
        compiler_params=small,
        name="solve",
    )(model_own, *tiles, place)
    tables = [solved]
    for s in (1, 2, 3):
        tables.append(lax.ppermute(solved, "stn", ring(s)))

    model = pl.pallas_call(
        model_kernel,
        out_shape=shape(4, 2 * rows, n),
        in_specs=[whole] * 5,
        out_specs=whole,
        scratch_shapes=[VMEM((8, 128), F32)],
        compiler_params=small,
        cost_estimate=pl.CostEstimate(flops=4 << 30, bytes_accessed=21 << 20, transcendentals=0),
        name="model",
    )(right_even, right_odd, left, model_own, place)

    gains, residual, changes = pl.pallas_call(
        residual_kernel,
        grid=(4,),
        out_shape=[shape(2, 4, rows), shape(2, 4, rows, n, dtype=BF16), shape(ITERS, 4)],
        in_specs=[whole] * 7,
        out_specs=[
            pl.BlockSpec((2, 4, rows), lambda q: (0, 0, 0)),
            pl.BlockSpec((2, 1, rows, n), lambda q: (0, q, 0, 0)),
            pl.BlockSpec((ITERS, 4), lambda q: (0, 0)),
        ],
        scratch_shapes=[VMEM((4, 8, n), F32)],
        compiler_params=small,
        name="residual",
    )(model, visibilities, *tables, place)
    return (gains, residual, changes)


def solution(mesh):
    placed = (P(None, "chan", "stn", None), P("chan"), P(None, "chan"), P(), P(), P(), P())

    return jax.shard_map(
        per_device,
        mesh=mesh,
        in_specs=placed,
        out_specs=(P(None, "chan", "stn"), P(None, "chan", "stn", None), P(None, "chan")),
        check_vma=False,
    )
```
